512 devices in a mesh: blk: 64 (over z, x), scale: 8 (over y, core).
Axes of the slice: x: 4, y: 4, z: 16, core: 2. Of those that a mesh axis runs over, the one named last changes fastest.
Arguments:
- start_block: float32 [64, 524288], P(None, ('blk', 'scale')), may hold values from -90 to 90
- blocks: bfloat16 [16384, 128, 128], P(('blk', 'scale')), may hold values from -0.1875 to 0.1875
- block_column: int32 [16384], P(('blk', 'scale')), may hold values from 0 to 7
- block_target: int32 [16384], P(('blk', 'scale')), may hold values from 0 to 15, as said below
- block_count: int32 [512], P(('blk', 'scale')), may hold values from 2 to 32, as said below
- partner: int32 [524288], P(('blk', 'scale')), may hold values from 0 to 1023, as said below
- degree: int32 [524288], P(('blk', 'scale')), may hold values from 1 to 16
Outputs:
- subspace: float32 [64, 524288], P(None, ('blk', 'scale'))
- rayleigh: float32 [64, 64], replicated
The draws below stay inside these ranges and needn't reach their ends.
Inputs may be any that keep to these rules, and one draw needn't show every extreme that they name: block_count[g] is the number of live slots of row group g; it is at least 2; some row group has all 32 slots live in every draw. In each row group, slots c < 2 have block_target of 8 or more, and all other slots have block_target below 8. Within each row group, partner is a permutation of 0 to 1023, and the pairing is mutual: if node i of group (b, s) has partner j, then node j of group (b, s xor 1) has partner i.
All inputs are finite; a program needn't handle non-finite values.
Results may differ from the reference program's by a relative error of at most 0.0011.
Values may be sent and summed in bfloat16 or wider, within the bound.
No kernel may reach another device: no remote copies, remote signals or barrier semaphores. Data moves between devices by JAX's collectives and lax.ppermute only.
A program may use at most 64 MiB of HBM per device.

```python
import jax
import jax.numpy as jnp
from jax import lax

K = 64
BLOCK = 128
R_DEV = 1024
CAP = 32
ITERS = 2
RB = 8
CROSS = 2
TILE_GROUPS = 64
SCALE_GROUPS = 8
NODES = 524288
SLOTS = 16384


def draw_start_block(key, part):
    key_base, key_cols, key_rows = jax.random.split(jax.random.fold_in(key, 11), 3)
    position = jnp.arange(NODES).astype(jnp.float32) / NODES
    col_scale = 10.0 ** (jax.random.uniform(key_cols, (1, NODES), jnp.float32) - 0.5)
    row_scale = 10.0 ** (jax.random.uniform(key_rows, (K, 1), jnp.float32) - 0.5)
    base = jax.random.truncated_normal(key_base, -4.0, 4.0, (K, NODES), jnp.float32)
    ramp = (1.0 + 2.0 * position) / 2.0
    return (base * row_scale * col_scale * ramp[None, :]).astype(jnp.float32)


def draw_block_target(key, part):
    groups = TILE_GROUPS * SCALE_GROUPS
    key_near, key_far = jax.random.split(jax.random.fold_in(key, 47), 2)
    near = jax.random.randint(key_near, (groups, CAP), 0, RB)
    far = jax.random.randint(key_far, (groups, CAP), RB, 2 * RB)
    slot_index = jnp.arange(CAP, dtype=jnp.int32)[None, :]
    return jnp.where(slot_index < CROSS, far, near).reshape(SLOTS).astype(jnp.int32)


def draw_block_count(key, part):
    groups = TILE_GROUPS * SCALE_GROUPS
    key_first, key_second, key_full = jax.random.split(jax.random.fold_in(key, 23), 3)
    first = jax.random.randint(key_first, (groups,), CROSS, CAP + 1)
    second = jax.random.randint(key_second, (groups,), CROSS, CAP + 1)
    fullest = jax.random.randint(key_full, (), 0, groups)
    return jnp.minimum(first, second).at[fullest].set(CAP).astype(jnp.int32)


def draw_partner(key, part):
    pairs = SCALE_GROUPS // 2
    scores = jax.random.randint(jax.random.fold_in(key, 37), (TILE_GROUPS, pairs, R_DEV), 0, 2 ** 19)
    scores = scores * R_DEV + jnp.arange(R_DEV, dtype=jnp.int32)[None, None, :]
    forward_map = jnp.argsort(scores, axis=-1).astype(jnp.int32)
    inverse_map = jnp.argsort(forward_map, axis=-1).astype(jnp.int32)
    joined = jnp.stack([forward_map, inverse_map], axis=2)
    return joined.reshape(NODES).astype(jnp.int32)


def set_ends(drawn, stream_key, low, high):
    dims = drawn.shape
    place = [jax.random.randint(jax.random.fold_in(stream_key, axis), (), 0, dims[axis]) for axis in range(len(dims))]
    drawn = drawn.at[tuple(place)].set(low)
    longest = dims.index(max(dims))
    place[longest] = (place[longest] + 1) % dims[longest]
    return drawn.at[tuple(place)].set(high)


def steps_of(key, extent, cuts, least, largest):
    gain, own = 1.0, jax.random.fold_in(key, 6)
    for dim, blocks in cuts:
        draws = jnp.exp(jax.random.uniform(jax.random.fold_in(own, dim), (blocks,), jnp.float32, least / len(cuts), largest / len(cuts)))
        gain = gain * jnp.repeat(draws, extent[dim] // blocks).reshape([-1 if axis == dim else 1 for axis in range(len(extent))])
    return gain


def bell_draw(key, extent, spread, most, pieces=(), kind=jnp.bfloat16):
    level = steps_of(key, extent, pieces, -0.22, 0.18) if pieces else 1.0
    entries = jax.random.normal(key, extent, jnp.float32) * spread * level
    return jnp.minimum(jnp.maximum(entries, -most), most).astype(kind)


def setup_inputs(seed: int = 0) -> dict:
    seeds = jax.random.split(jax.random.key(seed), 8)
    return {
        "start_block": draw_start_block(jax.random.fold_in(seeds[7], 71), 0),
        "blocks": bell_draw(seeds[1], (SLOTS, BLOCK, BLOCK), 1024 ** -0.5, 0.1875, ((0, 512),)),
        "block_column": set_ends(jax.random.randint(seeds[2], (SLOTS,), 0, RB), jax.random.fold_in(seeds[2], 1), 0, RB - 1).astype(jnp.int32),
        "block_target": draw_block_target(jax.random.fold_in(seeds[7], 71), 0),
        "block_count": draw_block_count(jax.random.fold_in(seeds[7], 71), 0),
        "partner": draw_partner(jax.random.fold_in(seeds[7], 71), 0),
        "degree": set_ends(jax.random.randint(seeds[6], (NODES,), 1, 17), jax.random.fold_in(seeds[6], 1), 1, 16).astype(jnp.int32),
    }


FULL_PRECISION = lax.Precision.HIGHEST

def cycle_terms(packed):
    own_vectors, next_vectors, weights, columns, targets, counts = packed
    row_blocks = R_DEV // 128
    live_mask = (jnp.arange(CAP)[None, :] < counts[:, None]).astype(jnp.float32)
    onecol = (columns[:, :, None] == jnp.arange(row_blocks)[None, None, :]).astype(jnp.float32) * live_mask[:, :, None]
    onetgt = (targets[:, :, None] == jnp.arange(2 * row_blocks)[None, None, :]).astype(jnp.float32) * live_mask[:, :, None]
    stacked = jnp.concatenate([own_vectors, next_vectors], axis=2).astype(jnp.float32)
    picked_cols = jnp.einsum('scr,skrj->sckj', onecol, own_vectors.astype(jnp.float32), precision=FULL_PRECISION)
    picked_tgts = jnp.einsum('sct,sktj->sckj', onetgt, stacked, precision=FULL_PRECISION)
    weights = weights.astype(jnp.float32)
    forward = jnp.einsum('scki,scji->sckj', picked_cols, weights, precision=FULL_PRECISION)
    backward = jnp.einsum('sckj,scji->scki', picked_tgts, weights, precision=FULL_PRECISION)
    nearby = jnp.einsum('scr,sckj->skrj', onetgt[:, :, :row_blocks], forward, precision=FULL_PRECISION)
    nearby = nearby + jnp.einsum('scr,sckj->skrj', onecol, backward, precision=FULL_PRECISION)
    ahead_sum = jnp.einsum('scr,sckj->skrj', onetgt[:, :, row_blocks:], forward, precision=FULL_PRECISION)
    return (nearby, ahead_sum)

def apply_operator(vectors, inv_sqrt_degree, blocks, block_column, block_target, block_count, partner):
    row_blocks = R_DEV // 128
    scaled = (vectors * inv_sqrt_degree[None, :]).astype(jnp.bfloat16)
    arranged = scaled.reshape(K, TILE_GROUPS, SCALE_GROUPS, row_blocks, 128).transpose(1, 2, 0, 3, 4)
    following = jnp.roll(arranged, -1, axis=0)
    packed = (arranged, following, blocks.reshape(TILE_GROUPS, SCALE_GROUPS, CAP, 128, 128), block_column.reshape(TILE_GROUPS, SCALE_GROUPS, CAP), block_target.reshape(TILE_GROUPS, SCALE_GROUPS, CAP), block_count.reshape(TILE_GROUPS, SCALE_GROUPS))
    nearby, ahead_sum = lax.map(cycle_terms, packed)
    surface = nearby + jnp.roll(ahead_sum, 1, axis=0)
    surface = surface.transpose(2, 0, 1, 3, 4).reshape(K, NODES)
    paired = scaled.reshape(K, TILE_GROUPS, SCALE_GROUPS // 2, 2, R_DEV)[:, :, :, ::-1, :]
    indices = jnp.broadcast_to(partner.reshape(1, TILE_GROUPS, SCALE_GROUPS // 2, 2, R_DEV), paired.shape)
    crossed = jnp.take_along_axis(paired, indices, axis=4).reshape(K, NODES).astype(jnp.float32)
    return vectors + inv_sqrt_degree[None, :] * (surface + crossed)

def orthonormal(images):
    gram_matrix = jnp.dot(images, images.T, precision=FULL_PRECISION) / NODES
    factor = jnp.linalg.cholesky(gram_matrix)
    factor_inverse = jax.scipy.linalg.solve_triangular(factor, jnp.eye(K, dtype=jnp.float32), lower=True)
    return jnp.dot(factor_inverse, images, precision=FULL_PRECISION)

def reference(start_block, blocks, block_column, block_target, block_count, partner, degree):
    inv_sqrt_degree = 1.0 / jnp.sqrt(degree.astype(jnp.float32))
    subspace = start_block
    for sweep_index in range(ITERS):
        subspace = orthonormal(apply_operator(subspace, inv_sqrt_degree, blocks, block_column, block_target, block_count, partner))
    images = apply_operator(subspace, inv_sqrt_degree, blocks, block_column, block_target, block_count, partner)
    rayleigh = jnp.dot(subspace, images.T, precision=FULL_PRECISION) / NODES
    return (subspace, rayleigh)
```

```python
import functools

import jax
import jax.numpy as jnp
from jax import lax
from jax.experimental import pallas as pl
from jax.experimental.pallas import tpu as pltpu
from jax.sharding import PartitionSpec as P

BLOCK = 128
CROSS = 2
ALONG_X = 4
BOTH = ("blk", "scale")
FULL = lax.Precision.HIGHEST
F32 = jnp.float32
BF16 = jnp.bfloat16

VMEM = pl.BlockSpec(memory_space=pltpu.VMEM)
SMEM = pl.BlockSpec(memory_space=pltpu.SMEM)


def lanes(j):
    return slice(j * BLOCK, (j + 1) * BLOCK)


def times(left, right):
    return jnp.dot(left, right, preferred_element_type=F32)


def times_t(left, right, precision=None):
    return lax.dot_general(
        left, right, (((1,), (1,)), ((), ())), precision=precision, preferred_element_type=F32
    )


def fold(product, k):
    return product if product.shape[0] == k else product[:k] + product[k:]


def split(value):
    high = value.astype(BF16)
    return jnp.concatenate([high, (value - high.astype(F32)).astype(BF16)], axis=0)


def first_kernel(x_ref, degree_ref, far_ref, col_ref, tgt_ref, dinv_ref, scaled_ref, ahead_ref, s3):
    k = x_ref.shape[0]
    dinv = 1.0 / jnp.sqrt(degree_ref[...].astype(F32))
    dinv_ref[...] = dinv
    scaled = (x_ref[...] * dinv).astype(BF16)
    scaled_ref[...] = scaled
    for j in range(s3.shape[0]):
        s3[j] = scaled[:, lanes(j)]
    for c in range(CROSS):
        ahead_ref[c * BLOCK : (c + 1) * BLOCK] = far_ref[c]
        at = CROSS * BLOCK + c * k
        ahead_ref[at : at + k] = s3[col_ref[c]]
        at = CROSS * (BLOCK + k) + c * 16
        row = jnp.full((16, BLOCK), tgt_ref[c] - s3.shape[0], jnp.int32)
        ahead_ref[at : at + 16] = row.astype(F32).astype(BF16)


def near_kernel(z_ref, blocks_ref, col_ref, tgt_ref, count_ref, out_ref, s3, acc):
    rb = s3.shape[0]
    k = out_ref.shape[0]
    for j in range(rb):
        s3[j] = z_ref[:, lanes(j)]
    acc[...] = jnp.zeros_like(acc)
    count = count_ref[0]
    for c in range(CROSS, blocks_ref.shape[0]):
        live = c < count
        column, target = col_ref[c], tgt_ref[c]
        weights = blocks_ref[c]
        forward = fold(times_t(s3[column], weights), k)
        backward = fold(times(s3[target], weights), k)
        acc[jnp.where(live, target, rb)] += forward
        acc[jnp.where(live, column, rb)] += backward
    for j in range(rb):
        out_ref[:, lanes(j)] = acc[j]


def crossed_block(part_ref, partner_ref, j, k):
    nodes = partner_ref.shape[1]
    ids = lax.broadcasted_iota(jnp.int32, (nodes, BLOCK), 0)
    onehot = jnp.where(ids == partner_ref[:, lanes(j)], 1.0, 0.0).astype(BF16)
    return fold(times(part_ref[...], onehot), k)


def finish_kernel(
    first,
    near_ref,
    v_ref,
    dinv_ref,
    next_ref,
    prev_ref,
    pay_ref,
    part_ref,
    partner_ref,
    far_ref,
    col_ref,
    tgt_ref,
    y_ref,
    z_ref,
    *rest,
):
    k = v_ref.shape[0]
    rb = v_ref.shape[1] // BLOCK
    back_ref, tot, z3 = rest[-3:]
    for j in range(rb):
        tot[j] = near_ref[:, lanes(j)] + crossed_block(part_ref, partner_ref, j, k)
    places = []
    for c in range(CROSS):
        at = CROSS * (BLOCK + k) + c * 16
        place = pay_ref[at : at + 16, :].astype(F32)[0:1]
        places.append(place)
        if first:
            theirs = next_ref[:, pl.ds(pl.multiple_of((tgt_ref[c] - rb) * BLOCK, BLOCK), BLOCK)]
            at = CROSS * BLOCK + c * k
            behind = pay_ref[at : at + k]
        else:
            theirs = next_ref[:, lanes(c)]
            behind = prev_ref[:, lanes(c)]
        tot[col_ref[c]] += fold(times(theirs, far_ref[c]), k)
        landed = fold(times_t(behind, pay_ref[c * BLOCK : (c + 1) * BLOCK]), k)
        for j in range(rb):
            tot[j] += jnp.where(place == j, landed, 0.0)
    for j in range(rb):
        dinv = dinv_ref[:, lanes(j)]
        y = v_ref[:, lanes(j)] + dinv * tot[j]
        z = split(y * dinv)
        y_ref[:, lanes(j)] = y
        z_ref[:, lanes(j)] = z
        z3[j] = z
    for c in range(CROSS):
        if first:
            rest[0][:, lanes(c)] = z3[col_ref[c]]
        wanted = jnp.zeros(z3.shape[1:], F32)
        for j in range(rb):
            wanted = jnp.where(places[c] == j, z3[j].astype(F32), wanted)
        back_ref[:, lanes(c)] = wanted.astype(BF16)


def form_kernel(
    y_ref, z_ref, blocks_ref, col_ref, tgt_ref, count_ref, u_ref, ufar_ref, gram_ref, s3, acc
):
    rb = s3.shape[0]
    k = u_ref.shape[0]
    for j in range(rb):
        s3[j] = z_ref[:, lanes(j)]
    acc[...] = jnp.zeros_like(acc)
    count = count_ref[0]
    for c in range(blocks_ref.shape[0]):
        forward = fold(times_t(s3[col_ref[c]], blocks_ref[c]), k)
        if c < CROSS:
            ufar_ref[:, lanes(c)] = forward
        else:
            acc[jnp.where(c < count, tgt_ref[c], rb)] += forward
    for j in range(rb):
        u_ref[:, lanes(j)] = acc[j]
    y = y_ref[...]
    gram_ref[...] = times_t(y, y, FULL)


def pair_kernel(u_ref, ufar_ref, gram_ref, y_ref, dinv_ref, next_ref, part_ref, partner_ref, out_ref):
    k = u_ref.shape[0]
    rb = u_ref.shape[1] // BLOCK
    left = [
        u_ref[:, lanes(j)] + 0.5 * crossed_block(part_ref, partner_ref, j, k) for j in range(rb)
    ]
    left.append(ufar_ref[...])
    theirs = next_ref[...].astype(F32)
    right = [y_ref[...] * dinv_ref[...], theirs[:k] + theirs[k:]]
    form = times_t(jnp.concatenate(left, axis=1), jnp.concatenate(right, axis=1), FULL)
    both = jnp.concatenate([gram_ref[...], form], axis=1)
    rows = out_ref.shape[1]
    for g in range(out_ref.shape[0]):
        out_ref[g] = both[g * rows : (g + 1) * rows]


def solve_kernel(nodes, both_ref, y_ref, sub_ref, ray_ref):
    k = y_ref.shape[0]
    pieces, rows, _ = both_ref.shape
    both = jnp.concatenate([both_ref[g] for g in range(pieces)], axis=0) * (1.0 / nodes)
    gram = both[:, :k]
    form = both[:, k:]
    projected = gram + form + form.T
    ids = lax.broadcasted_iota(jnp.int32, (k, 2 * k), 0)
    lane = lax.broadcasted_iota(jnp.int32, (k, 2 * k), 1)
    work = jnp.concatenate([gram, jnp.zeros((k, k), F32)], axis=1)
    work = jnp.where(lane == ids + k, 1.0, work)
    for i in range(k):
        row = work[i : i + 1]
        pivot = lax.rsqrt(work[i : i + 1, i : i + 1])
        row = row * pivot
        column = work[:, i : i + 1] * pivot
        work = jnp.where(ids > i, work - column * row, jnp.where(ids == i, row, work))
    inverse = work[:, k:]
    sub_ref[...] = jnp.dot(inverse, y_ref[...], precision=FULL, preferred_element_type=F32)
    half = jnp.dot(inverse, projected, precision=FULL, preferred_element_type=F32)
    ray_ref[...] = times_t(half, inverse, FULL)


def call(kernel, ins, outs, scratch, *args):
    return pl.pallas_call(
        kernel,
        out_shape=[jax.ShapeDtypeStruct(shape, dtype) for shape, dtype in outs],
        in_specs=ins,
        out_specs=[VMEM] * len(outs),
        scratch_shapes=scratch,
        compiler_params=pltpu.CompilerParams(vmem_limit_bytes=24 * 1024 * 1024),
    )(*args)


def shards(start_block, blocks, block_column, block_target, block_count, partner, degree):
    k, nodes = start_block.shape
    rb = nodes // BLOCK
    blk, scale = lax.axis_size("blk"), lax.axis_size("scale")
    total = blk * scale
    node_total = nodes * total
    degree = degree.reshape(1, nodes)
    partner = partner.reshape(1, nodes)

    def shifted(array, distance):
        return lax.ppermute(array, "blk", [(i, (i + distance) % blk) for i in range(blk)])

    def swapped(array):
        return lax.ppermute(array, "scale", [(i, i ^ 1) for i in range(scale)])

    far = blocks[:CROSS]
    pay_rows = CROSS * (BLOCK + k + 16)
    dinv, scaled, ahead = call(
        first_kernel,
        [VMEM, VMEM, VMEM, SMEM, SMEM],
        [((1, nodes), F32), ((k, nodes), BF16), ((pay_rows, BLOCK), BF16)],
        [pltpu.VMEM((rb, k, BLOCK), BF16)],
        start_block,
        degree,
        far,
        block_column,
        block_target,
    )

    def near(z):
        return call(
            near_kernel,
            [VMEM, VMEM, SMEM, SMEM, SMEM],
            [((k, nodes), F32)],
            [pltpu.VMEM((rb, z.shape[0], BLOCK), BF16), pltpu.VMEM((rb + 1, k, BLOCK), F32)],
            z,
            blocks,
            block_column,
            block_target,
            block_count,
        )[0]

    def finish(first, near_sum, v, from_next, from_prev, part):
        outs = [((k, nodes), F32), ((2 * k, nodes), BF16)]
        outs += [((2 * k, CROSS * BLOCK), BF16)] * (2 if first else 1)
        return call(
            functools.partial(finish_kernel, first),
            [VMEM] * 9 + [SMEM, SMEM],
            outs,
            [pltpu.VMEM((rb, k, BLOCK), F32), pltpu.VMEM((rb, 2 * k, BLOCK), BF16)],
            near_sum,
            v,
            dinv,
            from_next,
            from_prev,
            pay,
            part,
            partner,
            far,
            block_column,
            block_target,
        )

    pay = shifted(ahead, 1)
    from_next = shifted(scaled, -1)
    part = swapped(scaled)
    first_image, z, ahead, back = finish(True, near(scaled), start_block, from_next, pay, part)

    from_prev = shifted(ahead, 1)
    from_next = shifted(back, -1)
    part = swapped(z)
    images, z, back = finish(False, near(z), first_image, from_next, from_prev, part)

    from_next = shifted(back, -1)
    part = swapped(z)
    u, ufar, gram = call(
        form_kernel,
        [VMEM, VMEM, VMEM, SMEM, SMEM, SMEM],
        [((k, nodes), F32), ((k, CROSS * BLOCK), F32), ((k, k), F32)],
        [pltpu.VMEM((rb, 2 * k, BLOCK), BF16), pltpu.VMEM((rb + 1, k, BLOCK), F32)],
        images,
        z,
        blocks,
        block_column,
        block_target,
        block_count,
    )
    plane = ALONG_X * scale
    depth = blk // ALONG_X
    rows = k // plane
    (mine,) = call(
        pair_kernel,
        [VMEM] * 8,
        [((plane, rows, 2 * k), F32)],
        [],
        u,
        ufar,
        gram,
        images,
        dinv,
        from_next,
        part,
        partner,
    )

    planes = [[z_at * plane + i for i in range(plane)] for z_at in range(depth)]
    columns = [[z_at * ALONG_X + x_at for z_at in range(depth)] for x_at in range(ALONG_X)]
    piece = lax.all_to_all(mine, BOTH, 0, 0, axis_index_groups=planes).sum(0)
    piece = jnp.broadcast_to(piece[None], (depth, rows, 2 * k))
    piece = lax.all_to_all(piece, "blk", 0, 0, axis_index_groups=columns).sum(0)
    piece = jnp.broadcast_to(piece[None], (plane, rows, 2 * k))
    both = lax.all_to_all(piece, BOTH, 0, 0, axis_index_groups=planes)

    return call(
        functools.partial(solve_kernel, node_total),
        [VMEM, VMEM],
        [((k, nodes), F32), ((k, k), F32)],
        [],
        both,
        images,
    )


def solution(mesh):
    return jax.shard_map(
        shards,
        mesh=mesh,
        in_specs=(
            P(None, BOTH),
            P(BOTH, None, None),
            P(BOTH),
            P(BOTH),
            P(BOTH),
            P(BOTH),
            P(BOTH),
        ),
        out_specs=(P(None, BOTH), P()),
        check_vma=False,
    )
```

```python
import functools

import jax
import jax.numpy as jnp
from jax import lax
from jax.experimental import pallas as pl
from jax.experimental.pallas import tpu as pltpu
from jax.sharding import PartitionSpec as P


BLOCK = 128
CROSS = 2
ALONG_X = 4
SUBLANES = 8
PANEL = 8
BOTH = ("blk", "scale")
FULL = lax.Precision.HIGHEST
F32 = jnp.float32
BF16 = jnp.bfloat16

VMEM = pl.BlockSpec(memory_space=pltpu.VMEM)
SMEM = pl.BlockSpec(memory_space=pltpu.SMEM)


def lanes(j):
    return slice(j * BLOCK, (j + 1) * BLOCK)


def times(left, right):
    return jnp.dot(left, right, preferred_element_type=F32)


def times_t(left, right, precision=None):
    return lax.dot_general(
        left, right, (((1,), (1,)), ((), ())), precision=precision, preferred_element_type=F32
    )


def fold(product, k):
    return product if product.shape[0] == k else product[:k] + product[k:]


def split(value):
    high = value.astype(BF16)
    return jnp.concatenate([high, (value - high.astype(F32)).astype(BF16)], axis=0)


def first_kernel(
    x_hbm,
    degree_hbm,
    blocks_hbm,
    col_hbm,
    tgt_hbm,
    dinv_ref,
    scaled_ref,
    ahead_ref,
    blocks_ref,
    col_ref,
    tgt_ref,
    x_ref,
    degree_ref,
    s3,
    sems,
):
    k = x_ref.shape[0]
    far, near = pl.ds(0, CROSS), pl.ds(CROSS, blocks_ref.shape[0] - CROSS)
    moves = [
        (degree_hbm, degree_ref),
        (x_hbm, x_ref),
        (col_hbm, col_ref),
        (tgt_hbm, tgt_ref),
        (blocks_hbm.at[far], blocks_ref.at[far]),
        (blocks_hbm.at[near], blocks_ref.at[near]),
    ]
    copies = [pltpu.make_async_copy(src, dst, sems.at[i]) for i, (src, dst) in enumerate(moves)]
    for copy in copies:
        copy.start()
    for copy in copies[:5]:
        copy.wait()
    dinv = 1.0 / jnp.sqrt(degree_ref[...].astype(F32))
    dinv_ref[...] = dinv
    scaled = (x_ref[...] * dinv).astype(BF16)
    scaled_ref[...] = scaled
    for j in range(s3.shape[0]):
        s3[j] = scaled[:, lanes(j)]
    for c in range(CROSS):
        ahead_ref[c * BLOCK : (c + 1) * BLOCK] = blocks_ref[c]
        at = CROSS * BLOCK + c * k
        ahead_ref[at : at + k] = s3[col_ref[c]]
        at = CROSS * (BLOCK + k) + c * 16
        row = jnp.full((16, BLOCK), tgt_ref[c] - s3.shape[0], jnp.int32)
        ahead_ref[at : at + 16] = row.astype(F32).astype(BF16)
    copies[5].wait()


def near_kernel(z_ref, blocks_ref, col_ref, tgt_ref, count_ref, out_ref, s3, acc):
    rb = s3.shape[0]
    k = out_ref.shape[0]
    for j in range(rb):
        s3[j] = z_ref[:, lanes(j)]
    acc[...] = jnp.zeros_like(acc)
    count = count_ref[0]
    for c in range(CROSS, blocks_ref.shape[0]):
        live = c < count
        column, target = col_ref[c], tgt_ref[c]
        weights = blocks_ref[c]
        forward = fold(times_t(s3[column], weights), k)
        backward = fold(times(s3[target], weights), k)
        acc[jnp.where(live, target, rb)] += forward
        acc[jnp.where(live, column, rb)] += backward
    for j in range(rb):
        out_ref[:, lanes(j)] = acc[j]


def crossed_block(part_ref, partner_ref, j, k):
    nodes = partner_ref.shape[1]
    ids = lax.broadcasted_iota(jnp.int32, (nodes, BLOCK), 0)
    onehot = jnp.where(ids == partner_ref[:, lanes(j)], 1.0, 0.0).astype(BF16)
    return fold(times(part_ref[...], onehot), k)


def finish_kernel(
    first,
    near_ref,
    v_ref,
    dinv_ref,
    next_ref,
    prev_ref,
    pay_ref,
    part_ref,
    partner_ref,
    far_ref,
    col_ref,
    tgt_ref,
    y_ref,
    z_ref,
    *rest,
):
    k = v_ref.shape[0]
    rb = v_ref.shape[1] // BLOCK
    back_ref, tot, z3 = rest[-3:]
    for j in range(rb):
        tot[j] = near_ref[:, lanes(j)] + crossed_block(part_ref, partner_ref, j, k)
    places = []
    for c in range(CROSS):
        at = CROSS * (BLOCK + k) + c * 16
        place = pay_ref[at : at + 16, :].astype(F32)[0:1]
        places.append(place)
        if first:
            theirs = next_ref[:, pl.ds(pl.multiple_of((tgt_ref[c] - rb) * BLOCK, BLOCK), BLOCK)]
            at = CROSS * BLOCK + c * k
            behind = pay_ref[at : at + k]
        else:
            theirs = next_ref[:, lanes(c)]
            behind = prev_ref[:, lanes(c)]
        tot[col_ref[c]] += fold(times(theirs, far_ref[c]), k)
        landed = fold(times_t(behind, pay_ref[c * BLOCK : (c + 1) * BLOCK]), k)
        for j in range(rb):
            tot[j] += jnp.where(place == j, landed, 0.0)
    for j in range(rb):
        dinv = dinv_ref[:, lanes(j)]
        y = v_ref[:, lanes(j)] + dinv * tot[j]
        z = split(y * dinv)
        y_ref[:, lanes(j)] = y
        z_ref[:, lanes(j)] = z
        z3[j] = z
    for c in range(CROSS):
        if first:
            rest[0][:, lanes(c)] = z3[col_ref[c]]
        wanted = jnp.zeros(z3.shape[1:], F32)
        for j in range(rb):
            wanted = jnp.where(places[c] == j, z3[j].astype(F32), wanted)
        back_ref[:, lanes(c)] = wanted.astype(BF16)


def form_kernel(
    y_ref, z_ref, dinv_ref, blocks_ref, partner_ref, col_ref, tgt_ref, count_ref, right_ref, out_ref, s3, acc
):
    rb = s3.shape[0]
    k = y_ref.shape[0]
    for j in range(rb):
        s3[j] = z_ref[:, lanes(j)]
    acc[...] = jnp.zeros_like(acc)
    count = count_ref[0]
    for c in range(blocks_ref.shape[0]):
        forward = fold(times_t(s3[col_ref[c]], blocks_ref[c]), k)
        if c < CROSS:
            right_ref[:, lanes(rb + c)] = forward
        else:
            acc[jnp.where(c < count, tgt_ref[c], rb)] += forward
    nodes = y_ref.shape[1]
    for j in range(rb):
        ids = lax.broadcasted_iota(jnp.int32, (BLOCK, nodes), 0) + j * BLOCK
        onehot = jnp.where(ids == partner_ref[...], 0.5, 0.0).astype(BF16)
        right_ref[:, lanes(j)] = fold(times_t(z_ref[...], onehot), k)
    y = y_ref[...]
    z = y * dinv_ref[...]
    near = jnp.concatenate([acc[j] for j in range(rb)], axis=1)
    out_ref[:, :k] = times_t(y, y, FULL)
    out_ref[:, k:] = times_t(near, z, FULL)


def pair_kernel(right_ref, sums_ref, next_ref, part_ref, out_ref):
    k = right_ref.shape[0]
    theirs = jnp.concatenate([part_ref[...], next_ref[...]], axis=1).astype(F32)
    form = times_t(theirs[:k] + theirs[k:], right_ref[...], FULL)
    both = sums_ref[...] + jnp.concatenate([jnp.zeros((k, k), F32), form], axis=1)
    rows = out_ref.shape[1]
    for g in range(out_ref.shape[0]):
        out_ref[g] = both[g * rows : (g + 1) * rows]


def inverse_factor(gram):
    k = gram.shape[0]
    row_ids = lax.broadcasted_iota(jnp.int32, (SUBLANES, 2 * k), 0)
    lane = lax.broadcasted_iota(jnp.int32, (SUBLANES, 2 * k), 1)
    padded = jnp.concatenate([gram, jnp.zeros((k, k), F32)], axis=1)
    tiles = []
    for t in range(k // SUBLANES):
        tile = padded[t * SUBLANES : (t + 1) * SUBLANES]
        tiles.append(jnp.where(lane == row_ids + (k + t * SUBLANES), 1.0, tile))
    for start in range(0, k, PANEL):
        top, offset = divmod(start, SUBLANES)
        below = range(top, len(tiles))
        columns, rows = [], []
        for j in range(PANEL):
            at = start + j
            columns.append(
                {t: jnp.broadcast_to(tiles[t][:, at : at + 1], (SUBLANES, 2 * k)) for t in below}
            )
            rows.append(tiles[top][offset + j : offset + j + 1])
        for j in range(PANEL):
            pivot = lax.rsqrt(columns[j][top][offset + j : offset + j + 1])
            rows[j] = rows[j] * pivot
            columns[j] = {t: c * pivot for t, c in columns[j].items()}
            for m in range(j + 1, PANEL):
                factor = columns[j][top][offset + m : offset + m + 1]
                rows[m] = rows[m] - rows[j] * factor
                columns[m] = {t: c - columns[j][t] * factor for t, c in columns[m].items()}
        for t in below:
            if t == top and offset + PANEL == SUBLANES:
                continue
            tile = tiles[t]
            for j in range(PANEL):
                tile = tile - columns[j][t] * rows[j]
            if t == top:
                tile = jnp.where(row_ids >= offset + PANEL, tile, tiles[t])
            tiles[t] = tile
        for j in range(PANEL):
            tiles[top] = jnp.where(row_ids == offset + j, rows[j], tiles[top])
    return jnp.concatenate([tile[:, k:] for tile in tiles], axis=0)


def solve_kernel(nodes, both_ref, y_ref, sub_ref, ray_ref):
    k = y_ref.shape[0]
    pieces, _, _ = both_ref.shape
    both = jnp.concatenate([both_ref[g] for g in range(pieces)], axis=0) * (1.0 / nodes)
    gram = both[:, :k]
    form = both[:, k:]
    projected = gram + form + form.T
    inverse = inverse_factor(gram)
    sub_ref[...] = jnp.dot(inverse, y_ref[...], precision=FULL, preferred_element_type=F32)
    half = jnp.dot(inverse, projected, precision=FULL, preferred_element_type=F32)
    ray_ref[...] = times_t(half, inverse, FULL)


def call(kernel, ins, outs, scratch, *args, out_specs=None):
    return pl.pallas_call(
        kernel,
        out_shape=[jax.ShapeDtypeStruct(shape, dtype) for shape, dtype in outs],
        in_specs=ins,
        out_specs=[VMEM] * len(outs) if out_specs is None else out_specs,
        scratch_shapes=scratch,
        compiler_params=pltpu.CompilerParams(vmem_limit_bytes=24 * 1024 * 1024),
    )(*args)


def shards(start_block, blocks, block_column, block_target, block_count, partner, degree):
    k, nodes = start_block.shape
    rb = nodes // BLOCK
    blk, scale = lax.axis_size("blk"), lax.axis_size("scale")
    node_total = nodes * blk * scale
    degree = degree.reshape(1, nodes)
    partner = partner.reshape(1, nodes)

    def shifted(array, distance):
        return lax.ppermute(array, "blk", [(i, (i + distance) % blk) for i in range(blk)])

    def swapped(array):
        return lax.ppermute(array, "scale", [(i, i ^ 1) for i in range(scale)])

    pay_rows = CROSS * (BLOCK + k + 16)
    dinv, scaled, ahead, blocks, column, target = call(
        first_kernel,
        [pl.BlockSpec(memory_space=pltpu.HBM)] * 5,
        [
            ((1, nodes), F32),
            ((k, nodes), BF16),
            ((pay_rows, BLOCK), BF16),
            (blocks.shape, BF16),
            (block_column.shape, jnp.int32),
            (block_target.shape, jnp.int32),
        ],
        [
            pltpu.VMEM((k, nodes), F32),
            pltpu.VMEM((1, nodes), jnp.int32),
            pltpu.VMEM((rb, k, BLOCK), BF16),
            pltpu.SemaphoreType.DMA((6,)),
        ],
        *[
            pltpu.with_memory_space_constraint(array, pltpu.HBM)
            for array in (start_block, degree, blocks, block_column, block_target)
        ],
        out_specs=[VMEM] * 4 + [SMEM] * 2,
    )

    def near(z):
        return call(
            near_kernel,
            [VMEM, VMEM, SMEM, SMEM, SMEM],
            [((k, nodes), F32)],
            [pltpu.VMEM((rb, z.shape[0], BLOCK), BF16), pltpu.VMEM((rb + 1, k, BLOCK), F32)],
            z,
            blocks,
            column,
            target,
            block_count,
        )[0]

    def finish(first, near_sum, v, from_next, from_prev, part):
        outs = [((k, nodes), F32), ((2 * k, nodes), BF16)]
        outs += [((2 * k, CROSS * BLOCK), BF16)] * (2 if first else 1)
        return call(
            functools.partial(finish_kernel, first),
            [VMEM] * 9 + [SMEM, SMEM],
            outs,
            [pltpu.VMEM((rb, k, BLOCK), F32), pltpu.VMEM((rb, 2 * k, BLOCK), BF16)],
            near_sum,
            v,
            dinv,
            from_next,
            from_prev,
            pay,
            part,
            partner,
            blocks,
            column,
            target,
        )

    pay = shifted(ahead, 1)
    from_next = shifted(scaled, -1)
    part = swapped(scaled)
    first_image, z, ahead, back = finish(True, near(scaled), start_block, from_next, pay, part)

    from_prev = shifted(ahead, 1)
    from_next = shifted(back, -1)
    part = swapped(z)
    images, z, back = finish(False, near(z), first_image, from_next, from_prev, part)

    from_next = shifted(back, -1)
    part = swapped(z)
    right, sums = call(
        form_kernel,
        [VMEM] * 5 + [SMEM] * 3,
        [((k, nodes + CROSS * BLOCK), F32), ((k, 2 * k), F32)],
        [pltpu.VMEM((rb, 2 * k, BLOCK), BF16), pltpu.VMEM((rb + 1, k, BLOCK), F32)],
        images,
        z,
        dinv,
        blocks,
        partner,
        column,
        target,
        block_count,
    )
    plane = ALONG_X * scale
    depth = blk // ALONG_X
    rows = k // plane
    (mine,) = call(
        pair_kernel,
        [VMEM] * 4,
        [((plane, rows, 2 * k), F32)],
        [],
        right,
        sums,
        from_next,
        part,
    )

    planes = [[z_at * plane + i for i in range(plane)] for z_at in range(depth)]
    columns = [[z_at * ALONG_X + x_at for z_at in range(depth)] for x_at in range(ALONG_X)]
    piece = lax.all_to_all(mine, BOTH, 0, 0, axis_index_groups=planes).sum(0)
    piece = jnp.broadcast_to(piece[None], (depth, rows, 2 * k))
    piece = lax.all_to_all(piece, "blk", 0, 0, axis_index_groups=columns).sum(0)
    piece = jnp.broadcast_to(piece[None], (plane, rows, 2 * k))
    both = lax.all_to_all(piece, BOTH, 0, 0, axis_index_groups=planes)

    return call(
        functools.partial(solve_kernel, node_total),
        [VMEM, VMEM],
        [((k, nodes), F32), ((k, k), F32)],
        [],
        both,
        images,
    )


def layered(*args):
    return tuple(shards(*args))


def solution(mesh):
    return jax.shard_map(
        layered,
        mesh=mesh,
        in_specs=(
            P(None, BOTH),
            P(BOTH, None, None),
            P(BOTH),
            P(BOTH),
            P(BOTH),
            P(BOTH),
            P(BOTH),
        ),
        out_specs=(P(None, BOTH), P()),
        check_vma=False,
    )
```

```python
import functools

import jax
import jax.numpy as jnp
from jax import lax
from jax.experimental import pallas as pl
from jax.experimental.pallas import tpu as pltpu
from jax.sharding import PartitionSpec as P


BLOCK = 128
CROSS = 2
ALONG_X = 4
SUBLANES = 8
TILE_ROWS = 16
PANEL = 8
BOTH = ("blk", "scale")
FULL = lax.Precision.HIGHEST
F32 = jnp.float32
BF16 = jnp.bfloat16

VMEM = pl.BlockSpec(memory_space=pltpu.VMEM)
SMEM = pl.BlockSpec(memory_space=pltpu.SMEM)


def lanes(j):
    return slice(j * BLOCK, (j + 1) * BLOCK)


def times(left, right):
    return jnp.dot(left, right, preferred_element_type=F32)


def times_t(left, right, precision=None):
    return lax.dot_general(
        left, right, (((1,), (1,)), ((), ())), precision=precision, preferred_element_type=F32
    )


def fold(product, k):
    return product if product.shape[0] == k else product[:k] + product[k:]


def split(value):
    high = value.astype(BF16)
    return jnp.concatenate([high, (value - high.astype(F32)).astype(BF16)], axis=0)


def even_group():
    return lax.rem(lax.axis_index("blk"), 2) == 0


def first_kernel(
    x_hbm,
    degree_hbm,
    blocks_hbm,
    col_hbm,
    tgt_hbm,
    dinv_ref,
    scaled_ref,
    inner_ref,
    outer_ref,
    blocks_ref,
    col_ref,
    tgt_ref,
    x_ref,
    degree_ref,
    ahead_ref,
    sems,
):
    rb, k, _ = scaled_ref.shape
    far, near = pl.ds(0, CROSS), pl.ds(CROSS, blocks_ref.shape[0] - CROSS)
    moves = [
        (degree_hbm, degree_ref),
        (x_hbm, x_ref),
        (col_hbm, col_ref),
        (tgt_hbm, tgt_ref),
        (blocks_hbm.at[far], blocks_ref.at[far]),
        (blocks_hbm.at[near], blocks_ref.at[near]),
    ]
    copies = [pltpu.make_async_copy(src, dst, sems.at[i]) for i, (src, dst) in enumerate(moves)]
    for copy in copies:
        copy.start()
    for copy in copies[:5]:
        copy.wait()
    dinv = 1.0 / jnp.sqrt(degree_ref[...].astype(F32))
    dinv_ref[...] = dinv
    for j in range(rb):
        scaled_ref[j] = (x_ref[:, lanes(j)] * dinv[:, lanes(j)]).astype(BF16)
    rows, picks, places = payload_rows(k)
    ahead_ref[...] = jnp.zeros_like(ahead_ref)
    for c in range(CROSS):
        ahead_ref[rows[c]] = blocks_ref[c]
        ahead_ref[picks[c]] = scaled_ref[col_ref[c]]
        place = jnp.full((TILE_ROWS, BLOCK), tgt_ref[c] - rb, jnp.int32)
        ahead_ref[places[c]] = place.astype(F32).astype(BF16)
    even = even_group()
    ahead = ahead_ref[...]
    back = jnp.concatenate([scaled_ref[j] for j in range(rb)], axis=0)
    inner_ref[...] = jnp.where(even, ahead, back)
    outer_ref[...] = jnp.where(even, back, ahead)
    copies[5].wait()


def payload_rows(k):
    sizes = [BLOCK] * CROSS + [k] * CROSS + [TILE_ROWS] * CROSS
    starts = [sum(sizes[:i]) for i in range(len(sizes))]
    spans = [slice(at, at + size) for at, size in zip(starts, sizes)]
    return spans[:CROSS], spans[CROSS : 2 * CROSS], spans[2 * CROSS :]


def near_kernel(z_ref, blocks_ref, col_ref, tgt_ref, count_ref, out_ref, acc):
    rb, k, _ = out_ref.shape
    acc[...] = jnp.zeros_like(acc)
    count = count_ref[0]
    for c in range(CROSS, blocks_ref.shape[0]):
        live = c < count
        column, target = col_ref[c], tgt_ref[c]
        weights = blocks_ref[c]
        forward = fold(times_t(z_ref[column], weights), k)
        backward = fold(times(z_ref[target], weights), k)
        acc[jnp.where(live, target, rb)] += forward
        acc[jnp.where(live, column, rb)] += backward
    for j in range(rb):
        out_ref[j] = acc[j]


def side_by_side(ref):
    return jnp.concatenate([ref[j] for j in range(ref.shape[0])], axis=1)


def crossed_block(part_ref, partner_ref, j, k):
    nodes = partner_ref.shape[1]
    ids = lax.broadcasted_iota(jnp.int32, (nodes, BLOCK), 0)
    onehot = jnp.where(ids == partner_ref[:, lanes(j)], 1.0, 0.0).astype(BF16)
    return fold(times(side_by_side(part_ref), onehot), k)


def finish_kernel(
    first,
    near_ref,
    v_ref,
    dinv_ref,
    inner_ref,
    outer_ref,
    pay_inner_ref,
    pay_outer_ref,
    part_ref,
    partner_ref,
    blocks_ref,
    col_ref,
    tgt_ref,
    y_ref,
    z_ref,
    *rest,
):
    sends, (tot,) = rest[:-1], rest[-1:]
    k = v_ref.shape[0]
    rb = v_ref.shape[1] // BLOCK
    even = even_group()
    for j in range(rb):
        tot[j] = near_ref[j] + crossed_block(part_ref, partner_ref, j, k)
    rows, picks, spots = payload_rows(k)
    places = []
    for c in range(CROSS):
        sent = jnp.where(even, pay_outer_ref[spots[c]], pay_inner_ref[spots[c]])
        places.append(sent.astype(F32)[0:1])
        if first:
            at = pl.ds(pl.multiple_of((tgt_ref[c] - rb) * k, k), k)
            theirs = jnp.where(even, inner_ref[at], outer_ref[at])
            behind = jnp.where(even, pay_outer_ref[picks[c]], pay_inner_ref[picks[c]])
        else:
            theirs = jnp.where(even, inner_ref[:, lanes(c)], outer_ref[:, lanes(c)])
            behind = jnp.where(even, outer_ref[:, lanes(c)], inner_ref[:, lanes(c)])
        weights = jnp.where(even, pay_outer_ref[rows[c]], pay_inner_ref[rows[c]])
        tot[col_ref[c]] += fold(times(theirs, blocks_ref[c]), k)
        landed = fold(times_t(behind, weights), k)
        for j in range(rb):
            tot[j] += jnp.where(places[c] == j, landed, 0.0)
    for j in range(rb):
        dinv = dinv_ref[:, lanes(j)]
        y = v_ref[:, lanes(j)] + dinv * tot[j]
        y_ref[:, lanes(j)] = y
        z_ref[j] = split(y * dinv)
    for c in range(CROSS):
        wanted = jnp.zeros(z_ref.shape[1:], F32)
        for j in range(rb):
            wanted = jnp.where(places[c] == j, z_ref[j].astype(F32), wanted)
        back = wanted.astype(BF16)
        if first:
            ahead = z_ref[col_ref[c]]
            sends[0][:, lanes(c)] = jnp.where(even, ahead, back)
            sends[1][:, lanes(c)] = jnp.where(even, back, ahead)
        else:
            sends[0][:, lanes(c)] = back


def form_kernel(
    y_ref,
    z_ref,
    dinv_ref,
    blocks_ref,
    partner_ref,
    col_ref,
    tgt_ref,
    count_ref,
    right_ref,
    out_ref,
    acc,
):
    rb = z_ref.shape[0]
    k, nodes = y_ref.shape
    acc[...] = jnp.zeros_like(acc)
    count = count_ref[0]
    for c in range(blocks_ref.shape[0]):
        forward = fold(times_t(z_ref[col_ref[c]], blocks_ref[c]), k)
        if c < CROSS:
            right_ref[:, lanes(rb + c)] = forward
        else:
            acc[jnp.where(c < count, tgt_ref[c], rb)] += forward
    mine = side_by_side(z_ref)
    for j in range(rb):
        ids = lax.broadcasted_iota(jnp.int32, (BLOCK, nodes), 0) + j * BLOCK
        onehot = jnp.where(ids == partner_ref[...], 0.5, 0.0).astype(BF16)
        right_ref[:, lanes(j)] = fold(times_t(mine, onehot), k)
    y = y_ref[...]
    z = y * dinv_ref[...]
    near = jnp.concatenate([acc[j] for j in range(rb)], axis=1)
    out_ref[:, :k] = times_t(y, y, FULL)
    out_ref[:, k:] = times_t(near, z, FULL)


def pair_kernel(right_ref, sums_ref, next_ref, part_ref, out_ref):
    k = right_ref.shape[0]
    theirs = jnp.concatenate([side_by_side(part_ref), next_ref[...]], axis=1).astype(F32)
    form = times_t(theirs[:k] + theirs[k:], right_ref[...], FULL)
    both = sums_ref[...] + jnp.concatenate([jnp.zeros((k, k), F32), form], axis=1)
    rows = out_ref.shape[1]
    for g in range(out_ref.shape[0]):
        out_ref[g] = both[g * rows : (g + 1) * rows]


def inverse_factor(gram):
    k = gram.shape[0]
    row_ids = lax.broadcasted_iota(jnp.int32, (SUBLANES, 2 * k), 0)
    lane = lax.broadcasted_iota(jnp.int32, (SUBLANES, 2 * k), 1)
    padded = jnp.concatenate([gram, jnp.zeros((k, k), F32)], axis=1)
    tiles = []
    for t in range(k // SUBLANES):
        tile = padded[t * SUBLANES : (t + 1) * SUBLANES]
        tiles.append(jnp.where(lane == row_ids + (k + t * SUBLANES), 1.0, tile))
    for start in range(0, k, PANEL):
        top, offset = divmod(start, SUBLANES)
        below = range(top, len(tiles))
        columns, rows = [], []
        for j in range(PANEL):
            at = start + j
            columns.append(
                {t: jnp.broadcast_to(tiles[t][:, at : at + 1], (SUBLANES, 2 * k)) for t in below}
            )
            rows.append(tiles[top][offset + j : offset + j + 1])
        for j in range(PANEL):
            pivot = lax.rsqrt(columns[j][top][offset + j : offset + j + 1])
            rows[j] = rows[j] * pivot
            columns[j] = {t: c * pivot for t, c in columns[j].items()}
            for m in range(j + 1, PANEL):
                factor = columns[j][top][offset + m : offset + m + 1]
                rows[m] = rows[m] - rows[j] * factor
                columns[m] = {t: c - columns[j][t] * factor for t, c in columns[m].items()}
        for t in below:
            if t == top and offset + PANEL == SUBLANES:
                continue
            tile = tiles[t]
            for j in range(PANEL):
                tile = tile - columns[j][t] * rows[j]
            if t == top:
                tile = jnp.where(row_ids >= offset + PANEL, tile, tiles[t])
            tiles[t] = tile
        for j in range(PANEL):
            tiles[top] = jnp.where(row_ids == offset + j, rows[j], tiles[top])
    return jnp.concatenate([tile[:, k:] for tile in tiles], axis=0)


def solve_kernel(nodes, both_ref, y_ref, sub_ref, ray_ref):
    k = y_ref.shape[0]
    pieces, _, _ = both_ref.shape
    both = jnp.concatenate([both_ref[g] for g in range(pieces)], axis=0) * (1.0 / nodes)
    gram = both[:, :k]
    form = both[:, k:]
    projected = gram + form + form.T
    inverse = inverse_factor(gram)
    sub_ref[...] = jnp.dot(inverse, y_ref[...], precision=FULL, preferred_element_type=F32)
    half = jnp.dot(inverse, projected, precision=FULL, preferred_element_type=F32)
    ray_ref[...] = times_t(half, inverse, FULL)


def call(kernel, ins, outs, scratch, *args, out_specs=None):
    return pl.pallas_call(
        kernel,
        out_shape=[jax.ShapeDtypeStruct(shape, dtype) for shape, dtype in outs],
        in_specs=ins,
        out_specs=[VMEM] * len(outs) if out_specs is None else out_specs,
        scratch_shapes=scratch,
        compiler_params=pltpu.CompilerParams(vmem_limit_bytes=24 * 1024 * 1024),
    )(*args)


def shards(start_block, blocks, block_column, block_target, block_count, partner, degree):
    k, nodes = start_block.shape
    rb = nodes // BLOCK
    blk, scale = lax.axis_size("blk"), lax.axis_size("scale")
    node_total = nodes * blk * scale
    degree = degree.reshape(1, nodes)
    partner = partner.reshape(1, nodes)

    def moved(array, target):
        return lax.ppermute(array, "blk", [(i, target(i) % blk) for i in range(blk)])

    def swapped(array):
        return lax.ppermute(array, "scale", [(i, i ^ 1) for i in range(scale)])

    def inner(i):
        return i + 1 - 2 * (i % 2)

    def outer(i):
        return i - 1 + 2 * (i % 2)

    dinv, scaled, to_inner, to_outer, blocks, column, target = call(
        first_kernel,
        [pl.BlockSpec(memory_space=pltpu.HBM)] * 5,
        [
            ((1, nodes), F32),
            ((rb, k, BLOCK), BF16),
            ((rb * k, BLOCK), BF16),
            ((rb * k, BLOCK), BF16),
            (blocks.shape, BF16),
            (block_column.shape, jnp.int32),
            (block_target.shape, jnp.int32),
        ],
        [
            pltpu.VMEM((k, nodes), F32),
            pltpu.VMEM((1, nodes), jnp.int32),
            pltpu.VMEM((rb * k, BLOCK), BF16),
            pltpu.SemaphoreType.DMA((6,)),
        ],
        *[
            pltpu.with_memory_space_constraint(array, pltpu.HBM)
            for array in (start_block, degree, blocks, block_column, block_target)
        ],
        out_specs=[VMEM] * 5 + [SMEM] * 2,
    )

    def near(z):
        return call(
            near_kernel,
            [VMEM, VMEM, SMEM, SMEM, SMEM],
            [((rb, k, BLOCK), F32)],
            [pltpu.VMEM((rb + 1, k, BLOCK), F32)],
            z,
            blocks,
            column,
            target,
            block_count,
        )[0]

    def finish(first, near_sum, v, from_inner, from_outer, part):
        outs = [((k, nodes), F32), ((rb, 2 * k, BLOCK), BF16)]
        outs += [((2 * k, CROSS * BLOCK), BF16)] * (2 if first else 1)
        return call(
            functools.partial(finish_kernel, first),
            [VMEM] * 10 + [SMEM, SMEM],
            outs,
            [pltpu.VMEM((rb, k, BLOCK), F32)],
            near_sum,
            v,
            dinv,
            from_inner,
            from_outer,
            pay_inner,
            pay_outer,
            part,
            partner,
            blocks,
            column,
            target,
        )

    pay_outer = moved(to_outer, outer)
    pay_inner = moved(to_inner, inner)
    part = swapped(scaled)
    first_image, z, to_inner, to_outer = finish(
        True, near(scaled), start_block, pay_inner, pay_outer, part
    )

    from_outer = moved(to_outer, outer)
    from_inner = moved(to_inner, inner)
    part = swapped(z)
    images, z, back = finish(False, near(z), first_image, from_inner, from_outer, part)

    from_next = moved(back, lambda i: i - 1)
    part = swapped(z)
    right, sums = call(
        form_kernel,
        [VMEM] * 5 + [SMEM] * 3,
        [((k, nodes + CROSS * BLOCK), F32), ((k, 2 * k), F32)],
        [pltpu.VMEM((rb + 1, k, BLOCK), F32)],
        images,
        z,
        dinv,
        blocks,
        partner,
        column,
        target,
        block_count,
    )
    plane = ALONG_X * scale
    depth = blk // ALONG_X
    rows = k // plane
    (mine,) = call(
        pair_kernel,
        [VMEM] * 4,
        [((plane, rows, 2 * k), F32)],
        [],
        right,
        sums,
        from_next,
        part,
    )

    planes = [[z_at * plane + i for i in range(plane)] for z_at in range(depth)]
    columns = [[z_at * ALONG_X + x_at for z_at in range(depth)] for x_at in range(ALONG_X)]
    piece = lax.all_to_all(mine, BOTH, 0, 0, axis_index_groups=planes).sum(0)
    piece = jnp.broadcast_to(piece[None], (depth, rows, 2 * k))
    piece = lax.all_to_all(piece, "blk", 0, 0, axis_index_groups=columns).sum(0)
    piece = jnp.broadcast_to(piece[None], (plane, rows, 2 * k))
    both = lax.all_to_all(piece, BOTH, 0, 0, axis_index_groups=planes)

    return call(
        functools.partial(solve_kernel, node_total),
        [VMEM, VMEM],
        [((k, nodes), F32), ((k, k), F32)],
        [],
        both,
        images,
    )


def layered(*args):
    return tuple(shards(*args))


def solution(mesh):
    return jax.shard_map(
        layered,
        mesh=mesh,
        in_specs=(
            P(None, BOTH),
            P(BOTH, None, None),
            P(BOTH),
            P(BOTH),
            P(BOTH),
            P(BOTH),
            P(BOTH),
        ),
        out_specs=(P(None, BOTH), P()),
        check_vma=False,
    )
```

```python
import functools

import jax
import jax.numpy as jnp
from jax import lax
from jax.experimental import pallas as pl
from jax.experimental.pallas import tpu as pltpu
from jax.sharding import PartitionSpec as P


BLOCK = 128
CROSS = 2
ALONG_X = 4
SUBLANES = 8
TILE_ROWS = 16
WIDE = 256
PANEL = 8
BOTH = ("blk", "scale")
F32 = jnp.float32
BF16 = jnp.bfloat16

VMEM = pl.BlockSpec(memory_space=pltpu.VMEM)
SMEM = pl.BlockSpec(memory_space=pltpu.SMEM)


def lanes(j):
    return slice(j * BLOCK, (j + 1) * BLOCK)


def times(left, right):
    return jnp.dot(left, right, preferred_element_type=F32)


def times_t(left, right, precision=None):
    return lax.dot_general(
        left, right, (((1,), (1,)), ((), ())), precision=precision, preferred_element_type=F32
    )


def fold(product, k):
    return product if product.shape[0] == k else product[:k] + product[k:]


def split(value):
    high = value.astype(BF16)
    return jnp.concatenate([high, (value - high.astype(F32)).astype(BF16)], axis=0)


def even_group():
    return lax.rem(lax.axis_index("blk"), 2) == 0


def first_kernel(
    x_hbm,
    degree_hbm,
    blocks_hbm,
    col_hbm,
    tgt_hbm,
    dinv_ref,
    scaled_ref,
    inner_ref,
    outer_ref,
    blocks_ref,
    col_ref,
    tgt_ref,
    x_ref,
    degree_ref,
    ahead_ref,
    sems,
):
    rb, k, _ = scaled_ref.shape
    far, near = pl.ds(0, CROSS), pl.ds(CROSS, blocks_ref.shape[0] - CROSS)
    moves = [
        (degree_hbm, degree_ref),
        (x_hbm, x_ref),
        (col_hbm, col_ref),
        (tgt_hbm, tgt_ref),
        (blocks_hbm.at[far], blocks_ref.at[far]),
        (blocks_hbm.at[near], blocks_ref.at[near]),
    ]
    copies = [pltpu.make_async_copy(src, dst, sems.at[i]) for i, (src, dst) in enumerate(moves)]
    for copy in copies:
        copy.start()
    for copy in copies[:2]:
        copy.wait()
    dinv = 1.0 / jnp.sqrt(degree_ref[...].astype(F32))
    dinv_ref[...] = dinv
    for j in range(rb):
        scaled_ref[j] = (x_ref[:, lanes(j)] * dinv[:, lanes(j)]).astype(BF16)
    rows, picks, places = payload_rows(k)
    ahead_ref[...] = jnp.zeros_like(ahead_ref)
    for copy in copies[2:5]:
        copy.wait()
    for c in range(CROSS):
        ahead_ref[rows[c]] = blocks_ref[c]
        ahead_ref[picks[c]] = scaled_ref[col_ref[c]]
        place = jnp.full((TILE_ROWS, BLOCK), tgt_ref[c] - rb, jnp.int32)
        ahead_ref[places[c]] = place.astype(F32).astype(BF16)
    even = even_group()
    ahead = ahead_ref[...]
    back = jnp.concatenate([scaled_ref[j] for j in range(rb)], axis=0)
    inner_ref[...] = jnp.where(even, ahead, back)
    outer_ref[...] = jnp.where(even, back, ahead)
    copies[5].wait()


def payload_rows(k):
    sizes = [BLOCK] * CROSS + [k] * CROSS + [TILE_ROWS] * CROSS
    starts = [sum(sizes[:i]) for i in range(len(sizes))]
    spans = [slice(at, at + size) for at, size in zip(starts, sizes)]
    return spans[:CROSS], spans[CROSS : 2 * CROSS], spans[2 * CROSS :]


def diagonal(z_ref, place_ref, slots):
    first, second = z_ref[place_ref[slots[0]]], z_ref[place_ref[slots[1]]]
    zero = jnp.zeros_like(first)
    return jnp.concatenate(
        [jnp.concatenate([first, zero], axis=1), jnp.concatenate([zero, second], axis=1)], axis=0
    )


def across(blocks_ref, slots):
    return jnp.concatenate([blocks_ref[c] for c in slots], axis=1)


def down(blocks_ref, slots):
    return jnp.concatenate([blocks_ref[c] for c in slots], axis=0)


def near_kernel(z_ref, blocks_ref, col_ref, tgt_ref, count_ref, out_ref, acc):
    rb, k, _ = out_ref.shape
    acc[...] = jnp.zeros_like(acc)
    count = count_ref[0]
    slots = range(CROSS, blocks_ref.shape[0])

    def add(c, forward, backward):
        live = c < count
        acc[jnp.where(live, tgt_ref[c], rb)] += forward
        acc[jnp.where(live, col_ref[c], rb)] += backward

    if z_ref.shape[1] == k:
        for c in slots[::2]:
            pair = (c, c + 1)
            forward = times_t(diagonal(z_ref, col_ref, pair), across(blocks_ref, pair))
            backward = times(diagonal(z_ref, tgt_ref, pair), down(blocks_ref, pair))
            add(c, forward[:k], backward[:k])
            add(c + 1, forward[k:], backward[k:])
    else:
        for c in slots:
            weights = blocks_ref[c]
            forward = fold(times_t(z_ref[col_ref[c]], weights), k)
            add(c, forward, fold(times(z_ref[tgt_ref[c]], weights), k))
    for j in range(rb):
        out_ref[j] = acc[j]


def side_by_side(ref):
    return jnp.concatenate([ref[j] for j in range(ref.shape[0])], axis=1)


def crossed_blocks(part_ref, partner_ref, at, k):
    nodes = partner_ref.shape[1]
    ids = lax.broadcasted_iota(jnp.int32, (nodes, WIDE), 0)
    onehot = jnp.where(ids == partner_ref[:, at : at + WIDE], 1.0, 0.0).astype(BF16)
    return fold(times(side_by_side(part_ref), onehot), k)


def finish_kernel(
    first,
    near_ref,
    v_ref,
    dinv_ref,
    inner_ref,
    outer_ref,
    pay_inner_ref,
    pay_outer_ref,
    part_ref,
    partner_ref,
    blocks_ref,
    col_ref,
    tgt_ref,
    y_ref,
    z_ref,
    *rest,
):
    *sends, tot = rest
    k = v_ref.shape[0]
    rb = v_ref.shape[1] // BLOCK
    even = even_group()
    for at in range(0, rb * BLOCK, WIDE):
        crossed = crossed_blocks(part_ref, partner_ref, at, k)
        for i in range(WIDE // BLOCK):
            j = at // BLOCK + i
            tot[j] = near_ref[j] + crossed[:, lanes(i)]
    rows, picks, spots = payload_rows(k)
    places = []
    for c in range(CROSS):
        sent = jnp.where(even, pay_outer_ref[spots[c]], pay_inner_ref[spots[c]])
        places.append(sent.astype(F32)[0:1])
        if first:
            at = pl.ds(pl.multiple_of((tgt_ref[c] - rb) * k, k), k)
            theirs = jnp.where(even, inner_ref[at], outer_ref[at])
            behind = jnp.where(even, pay_outer_ref[picks[c]], pay_inner_ref[picks[c]])
        else:
            theirs = jnp.where(even, inner_ref[:, lanes(c)], outer_ref[:, lanes(c)])
            behind = jnp.where(even, outer_ref[:, lanes(c)], inner_ref[:, lanes(c)])
        weights = jnp.where(even, pay_outer_ref[rows[c]], pay_inner_ref[rows[c]])
        tot[col_ref[c]] += fold(times(theirs, blocks_ref[c]), k)
        landed = fold(times_t(behind, weights), k)
        for j in range(rb):
            tot[j] += jnp.where(places[c] == j, landed, 0.0)
    for j in range(rb):
        dinv = dinv_ref[:, lanes(j)]
        y = v_ref[:, lanes(j)] + dinv * tot[j]
        y_ref[:, lanes(j)] = y
        z_ref[j] = split(y * dinv)
        if not first:
            sends[1][j] = z_ref[j, :k]
    for c in range(CROSS):
        wanted = jnp.zeros(z_ref.shape[1:], F32)
        for j in range(rb):
            wanted = jnp.where(places[c] == j, z_ref[j].astype(F32), wanted)
        back = wanted.astype(BF16)
        if first:
            ahead = z_ref[col_ref[c]]
            sends[0][:, lanes(c)] = jnp.where(even, ahead, back)
            sends[1][:, lanes(c)] = jnp.where(even, back, ahead)
        else:
            sends[0][:, lanes(c)] = back[:k]


def form_kernel(
    y_ref,
    z_ref,
    dinv_ref,
    blocks_ref,
    partner_ref,
    col_ref,
    tgt_ref,
    count_ref,
    right_ref,
    sums_ref,
    parts_ref,
    acc,
):
    rb = z_ref.shape[0]
    k, nodes = y_ref.shape
    acc[...] = jnp.zeros_like(acc)
    count = count_ref[0]
    for c in range(blocks_ref.shape[0]):
        forward = fold(times_t(z_ref[col_ref[c]], blocks_ref[c]), k)
        if c < CROSS:
            right_ref[:, lanes(rb + c)] = split(forward)
        else:
            acc[jnp.where(c < count, tgt_ref[c], rb)] += forward
    mine = side_by_side(z_ref)
    for at in range(0, nodes, WIDE):
        ids = lax.broadcasted_iota(jnp.int32, (WIDE, nodes), 0) + at
        onehot = jnp.where(ids == partner_ref[...], 0.5, 0.0).astype(BF16)
        right_ref[:, at : at + WIDE] = times_t(mine, onehot).astype(BF16)
    for j in range(rb):
        parts_ref[:, lanes(j)] = split(y_ref[:, lanes(j)])
    near = [split(acc[j] * dinv_ref[:, lanes(j)]) for j in range(rb)]
    parts = parts_ref[...]
    left = jnp.concatenate([parts, jnp.concatenate(near, axis=1)], axis=0)
    both = halves_added(times_t(left, parts))
    sums_ref[:, :k] = both[:k]
    sums_ref[:, k:] = both[k:]


def halves_added(product):
    k = product.shape[1] // 2
    wide = product[:, :k] + product[:, k:]
    pairs = range(0, product.shape[0], 2 * k)
    return jnp.concatenate([wide[at : at + k] + wide[at + k : at + 2 * k] for at in pairs], axis=0)


def pair_kernel(right_ref, sums_ref, next_ref, part_ref, out_ref):
    k = sums_ref.shape[0]
    theirs = jnp.concatenate([side_by_side(part_ref), next_ref[...]], axis=1)
    product = times_t(theirs, right_ref[...])
    form = product[:, :k] + product[:, k:]
    both = sums_ref[...] + jnp.concatenate([jnp.zeros((k, k), F32), form], axis=1)
    rows = out_ref.shape[1]
    for g in range(out_ref.shape[0]):
        out_ref[g] = both[g * rows : (g + 1) * rows]


def inverse_factor(gram):
    k = gram.shape[0]
    row_ids = lax.broadcasted_iota(jnp.int32, (SUBLANES, 2 * k), 0)
    lane = lax.broadcasted_iota(jnp.int32, (SUBLANES, 2 * k), 1)
    padded = jnp.concatenate([gram, jnp.zeros((k, k), F32)], axis=1)
    tiles = []
    for t in range(k // SUBLANES):
        tile = padded[t * SUBLANES : (t + 1) * SUBLANES]
        tiles.append(jnp.where(lane == row_ids + (k + t * SUBLANES), 1.0, tile))
    for start in range(0, k, PANEL):
        top, offset = divmod(start, SUBLANES)
        below = range(top, len(tiles))
        columns, rows = [], []
        for j in range(PANEL):
            at = start + j
            columns.append(
                {t: jnp.broadcast_to(tiles[t][:, at : at + 1], (SUBLANES, 2 * k)) for t in below}
            )
            rows.append(tiles[top][offset + j : offset + j + 1])
        for j in range(PANEL):
            pivot = lax.rsqrt(columns[j][top][offset + j : offset + j + 1])
            rows[j] = rows[j] * pivot
            columns[j] = {t: c * pivot for t, c in columns[j].items()}
            for m in range(j + 1, PANEL):
                factor = columns[j][top][offset + m : offset + m + 1]
                rows[m] = rows[m] - rows[j] * factor
                columns[m] = {t: c - columns[j][t] * factor for t, c in columns[m].items()}
        for t in below:
            if t == top and offset + PANEL == SUBLANES:
                continue
            tile = tiles[t]
            for j in range(PANEL):
                tile = tile - columns[j][t] * rows[j]
            if t == top:
                tile = jnp.where(row_ids >= offset + PANEL, tile, tiles[t])
            tiles[t] = tile
        for j in range(PANEL):
            tiles[top] = jnp.where(row_ids == offset + j, rows[j], tiles[top])
    return jnp.concatenate([tile[:, k:] for tile in tiles], axis=0)


def solve_kernel(nodes, both_ref, parts_ref, sub_ref, ray_ref):
    k = sub_ref.shape[0]
    pieces, _, _ = both_ref.shape
    both = jnp.concatenate([both_ref[g] for g in range(pieces)], axis=0) * (1.0 / nodes)
    gram = both[:, :k]
    form = both[:, k:]
    projected = gram + form + form.T
    inverse = inverse_factor(gram)
    left = split(inverse)
    sub_ref[...] = fold(times(jnp.concatenate([left, left], axis=1), parts_ref[...]), k)
    half = fold(times(jnp.concatenate([left, left], axis=1), split(projected)), k)
    ray_ref[...] = halves_added(times_t(split(half), left))


def call(kernel, ins, outs, scratch, *args, out_specs=None):
    return pl.pallas_call(
        kernel,
        out_shape=[jax.ShapeDtypeStruct(shape, dtype) for shape, dtype in outs],
        in_specs=ins,
        out_specs=[VMEM] * len(outs) if out_specs is None else out_specs,
        scratch_shapes=scratch,
        compiler_params=pltpu.CompilerParams(vmem_limit_bytes=24 * 1024 * 1024),
    )(*args)


def shards(start_block, blocks, block_column, block_target, block_count, partner, degree):
    k, nodes = start_block.shape
    rb = nodes // BLOCK
    blk, scale = lax.axis_size("blk"), lax.axis_size("scale")
    node_total = nodes * blk * scale
    degree = degree.reshape(1, nodes)
    partner = partner.reshape(1, nodes)

    def moved(array, target):
        return lax.ppermute(array, "blk", [(i, target(i) % blk) for i in range(blk)])

    def swapped(array):
        return lax.ppermute(array, "scale", [(i, i ^ 1) for i in range(scale)])

    def inner(i):
        return i + 1 - 2 * (i % 2)

    def outer(i):
        return i - 1 + 2 * (i % 2)

    dinv, scaled, to_inner, to_outer, blocks, column, target = call(
        first_kernel,
        [pl.BlockSpec(memory_space=pltpu.HBM)] * 5,
        [
            ((1, nodes), F32),
            ((rb, k, BLOCK), BF16),
            ((rb * k, BLOCK), BF16),
            ((rb * k, BLOCK), BF16),
            (blocks.shape, BF16),
            (block_column.shape, jnp.int32),
            (block_target.shape, jnp.int32),
        ],
        [
            pltpu.VMEM((k, nodes), F32),
            pltpu.VMEM((1, nodes), jnp.int32),
            pltpu.VMEM((rb * k, BLOCK), BF16),
            pltpu.SemaphoreType.DMA((6,)),
        ],
        *[
            pltpu.with_memory_space_constraint(array, pltpu.HBM)
            for array in (start_block, degree, blocks, block_column, block_target)
        ],
        out_specs=[VMEM] * 5 + [SMEM] * 2,
    )

    def near(z):
        return call(
            near_kernel,
            [VMEM, VMEM, SMEM, SMEM, SMEM],
            [((rb, k, BLOCK), F32)],
            [pltpu.VMEM((rb + 1, k, BLOCK), F32)],
            z,
            blocks,
            column,
            target,
            block_count,
        )[0]

    def finish(first, near_sum, v, from_inner, from_outer, part):
        outs = [((k, nodes), F32), ((rb, 2 * k, BLOCK), BF16)]
        if first:
            outs += [((2 * k, CROSS * BLOCK), BF16)] * 2
        else:
            outs += [((k, CROSS * BLOCK), BF16), ((rb, k, BLOCK), BF16)]
        return call(
            functools.partial(finish_kernel, first),
            [VMEM] * 10 + [SMEM, SMEM],
            outs,
            [pltpu.VMEM((rb, k, BLOCK), F32)],
            near_sum,
            v,
            dinv,
            from_inner,
            from_outer,
            pay_inner,
            pay_outer,
            part,
            partner,
            blocks,
            column,
            target,
        )

    pay_outer = moved(to_outer, outer)
    pay_inner = moved(to_inner, inner)
    part = swapped(scaled)
    first_image, z, to_inner, to_outer = finish(
        True, near(scaled), start_block, pay_inner, pay_outer, part
    )

    from_outer = moved(to_outer, outer)
    from_inner = moved(to_inner, inner)
    part = swapped(z)
    images, z, back, high = finish(False, near(z), first_image, from_inner, from_outer, part)

    from_next = moved(back, lambda i: i - 1)
    part = swapped(high)
    right, sums, parts = call(
        form_kernel,
        [VMEM] * 5 + [SMEM] * 3,
        [((2 * k, nodes + CROSS * BLOCK), BF16), ((k, 2 * k), F32), ((2 * k, nodes), BF16)],
        [pltpu.VMEM((rb + 1, k, BLOCK), F32)],
        images,
        z,
        dinv,
        blocks,
        partner,
        column,
        target,
        block_count,
    )
    plane = ALONG_X * scale
    depth = blk // ALONG_X
    rows = k // plane
    (mine,) = call(
        pair_kernel,
        [VMEM] * 4,
        [((plane, rows, 2 * k), F32)],
        [],
        right,
        sums,
        from_next,
        part,
    )

    planes = [[z_at * plane + i for i in range(plane)] for z_at in range(depth)]
    columns = [[z_at * ALONG_X + x_at for z_at in range(depth)] for x_at in range(ALONG_X)]
    piece = lax.all_to_all(mine, BOTH, 0, 0, axis_index_groups=planes).sum(0)
    piece = jnp.broadcast_to(piece[None], (depth, rows, 2 * k))
    piece = lax.all_to_all(piece, "blk", 0, 0, axis_index_groups=columns).sum(0)
    piece = jnp.broadcast_to(piece[None], (plane, rows, 2 * k))
    both = lax.all_to_all(piece, BOTH, 0, 0, axis_index_groups=planes)

    return call(
        functools.partial(solve_kernel, node_total),
        [VMEM, VMEM],
        [((k, nodes), F32), ((k, k), F32)],
        [],
        both,
        parts,
    )


def layered(*args):
    return tuple(shards(*args))


def solution(mesh):
    return jax.shard_map(
        layered,
        mesh=mesh,
        in_specs=(
            P(None, BOTH),
            P(BOTH, None, None),
            P(BOTH),
            P(BOTH),
            P(BOTH),
            P(BOTH),
            P(BOTH),
        ),
        out_specs=(P(None, BOTH), P()),
        check_vma=False,
    )
```

```python
import functools

import jax
import jax.numpy as jnp
from jax import lax
from jax.experimental import pallas as pl
from jax.experimental.pallas import tpu as pltpu
from jax.sharding import PartitionSpec as P


BLOCK = 128
CROSS = 2
ALONG_X = 4
SUBLANES = 8
TILE_ROWS = 16
WIDE = 256
PANEL = 8
BOTH = ("blk", "scale")
F32 = jnp.float32
BF16 = jnp.bfloat16

VMEM = pl.BlockSpec(memory_space=pltpu.VMEM)
SMEM = pl.BlockSpec(memory_space=pltpu.SMEM)


def lanes(j):
    return slice(j * BLOCK, (j + 1) * BLOCK)


def times(left, right):
    return jnp.dot(left, right, preferred_element_type=F32)


def times_t(left, right, precision=None):
    return lax.dot_general(
        left, right, (((1,), (1,)), ((), ())), precision=precision, preferred_element_type=F32
    )


def fold(product, k):
    return product if product.shape[0] == k else product[:k] + product[k:]


def split(value):
    high = value.astype(BF16)
    return jnp.concatenate([high, (value - high.astype(F32)).astype(BF16)], axis=0)


def even_group():
    return lax.rem(lax.axis_index("blk"), 2) == 0


def first_kernel(
    x_hbm,
    degree_hbm,
    blocks_hbm,
    col_hbm,
    tgt_hbm,
    dinv_ref,
    scaled_ref,
    inner_ref,
    outer_ref,
    col_ref,
    tgt_ref,
    x_ref,
    degree_ref,
    ahead_ref,
    sems,
):
    rb, k, _ = scaled_ref.shape
    rows, picks, places = payload_rows(k)
    moves = [
        (degree_hbm, degree_ref),
        (x_hbm, x_ref),
        (col_hbm, col_ref),
        (tgt_hbm, tgt_ref),
    ]
    moves += [(blocks_hbm.at[c], ahead_ref.at[rows[c]]) for c in range(CROSS)]
    copies = [pltpu.make_async_copy(src, dst, sems.at[i]) for i, (src, dst) in enumerate(moves)]
    for copy in copies:
        copy.start()
    for copy in copies[:2]:
        copy.wait()
    dinv = 1.0 / jnp.sqrt(degree_ref[...].astype(F32))
    dinv_ref[...] = dinv
    for j in range(rb):
        scaled_ref[j] = (x_ref[:, lanes(j)] * dinv[:, lanes(j)]).astype(BF16)
    tail = places[-1].stop
    ahead_ref[tail:] = jnp.zeros_like(ahead_ref[tail:])
    for copy in copies[2:]:
        copy.wait()
    for c in range(CROSS):
        ahead_ref[picks[c]] = scaled_ref[col_ref[c]]
        place = jnp.full((TILE_ROWS, BLOCK), tgt_ref[c] - rb, jnp.int32)
        ahead_ref[places[c]] = place.astype(F32).astype(BF16)
    even = even_group()
    ahead = ahead_ref[...]
    back = jnp.concatenate([scaled_ref[j] for j in range(rb)], axis=0)
    inner_ref[...] = jnp.where(even, ahead, back)
    outer_ref[...] = jnp.where(even, back, ahead)


def payload_rows(k):
    sizes = [BLOCK] * CROSS + [k] * CROSS + [TILE_ROWS] * CROSS
    starts = [sum(sizes[:i]) for i in range(len(sizes))]
    spans = [slice(at, at + size) for at, size in zip(starts, sizes)]
    return spans[:CROSS], spans[CROSS : 2 * CROSS], spans[2 * CROSS :]


def diagonal(z_ref, place_ref, slots):
    first, second = z_ref[place_ref[slots[0]]], z_ref[place_ref[slots[1]]]
    zero = jnp.zeros_like(first)
    return jnp.concatenate(
        [jnp.concatenate([first, zero], axis=1), jnp.concatenate([zero, second], axis=1)], axis=0
    )


def across(blocks_ref, slots):
    return jnp.concatenate([blocks_ref[c] for c in slots], axis=1)


def down(blocks_ref, slots):
    return jnp.concatenate([blocks_ref[c] for c in slots], axis=0)


def near_kernel(z_ref, blocks_ref, col_ref, tgt_ref, count_ref, out_ref, acc):
    rb, k, _ = out_ref.shape
    acc[...] = jnp.zeros_like(acc)
    count = count_ref[0]
    slots = range(CROSS, blocks_ref.shape[0])

    def add(c, forward, backward):
        live = c < count
        acc[jnp.where(live, tgt_ref[c], rb)] += forward
        acc[jnp.where(live, col_ref[c], rb)] += backward

    if z_ref.shape[1] == k:
        for c in slots[::2]:
            pair = (c, c + 1)
            forward = times_t(diagonal(z_ref, col_ref, pair), across(blocks_ref, pair))
            backward = times(diagonal(z_ref, tgt_ref, pair), down(blocks_ref, pair))
            add(c, forward[:k], backward[:k])
            add(c + 1, forward[k:], backward[k:])
    else:
        for c in slots:
            weights = blocks_ref[c]
            forward = fold(times_t(z_ref[col_ref[c]], weights), k)
            add(c, forward, fold(times(z_ref[tgt_ref[c]], weights), k))
    for j in range(rb):
        out_ref[j] = acc[j]


def side_by_side(ref):
    return jnp.concatenate([ref[j] for j in range(ref.shape[0])], axis=1)


def crossed_blocks(part_ref, partner_ref, at, k):
    nodes = partner_ref.shape[1]
    ids = lax.broadcasted_iota(jnp.int32, (nodes, WIDE), 0)
    onehot = jnp.where(ids == partner_ref[:, at : at + WIDE], 1.0, 0.0).astype(BF16)
    return fold(times(side_by_side(part_ref), onehot), k)


def finish_kernel(
    first,
    near_ref,
    v_ref,
    dinv_ref,
    inner_ref,
    outer_ref,
    pay_inner_ref,
    pay_outer_ref,
    part_ref,
    partner_ref,
    blocks_ref,
    col_ref,
    tgt_ref,
    y_ref,
    z_ref,
    *rest,
):
    *sends, tot = rest
    k = v_ref.shape[0]
    rb = v_ref.shape[1] // BLOCK
    even = even_group()
    for at in range(0, rb * BLOCK, WIDE):
        crossed = crossed_blocks(part_ref, partner_ref, at, k)
        for i in range(WIDE // BLOCK):
            j = at // BLOCK + i
            tot[j] = near_ref[j] + crossed[:, lanes(i)]
    rows, picks, spots = payload_rows(k)
    places = []
    for c in range(CROSS):
        sent = jnp.where(even, pay_outer_ref[spots[c]], pay_inner_ref[spots[c]])
        places.append(sent.astype(F32)[0:1])
        if first:
            at = pl.ds(pl.multiple_of((tgt_ref[c] - rb) * k, k), k)
            theirs = jnp.where(even, inner_ref[at], outer_ref[at])
            behind = jnp.where(even, pay_outer_ref[picks[c]], pay_inner_ref[picks[c]])
        else:
            theirs = jnp.where(even, inner_ref[:, lanes(c)], outer_ref[:, lanes(c)])
            behind = jnp.where(even, outer_ref[:, lanes(c)], inner_ref[:, lanes(c)])
        weights = jnp.where(even, pay_outer_ref[rows[c]], pay_inner_ref[rows[c]])
        tot[col_ref[c]] += fold(times(theirs, blocks_ref[c]), k)
        landed = fold(times_t(behind, weights), k)
        for j in range(rb):
            tot[j] += jnp.where(places[c] == j, landed, 0.0)
    for j in range(rb):
        dinv = dinv_ref[:, lanes(j)]
        y = v_ref[:, lanes(j)] + dinv * tot[j]
        y_ref[:, lanes(j)] = y
        z_ref[j] = split(y * dinv)
        if not first:
            sends[1][j] = z_ref[j, :k]
    for c in range(CROSS):
        wanted = jnp.zeros(z_ref.shape[1:], F32)
        for j in range(rb):
            wanted = jnp.where(places[c] == j, z_ref[j].astype(F32), wanted)
        back = wanted.astype(BF16)
        ahead = z_ref[col_ref[c]]
        if first:
            sends[0][:, lanes(c)] = jnp.where(even, ahead, back)
            sends[1][:, lanes(c)] = jnp.where(even, back, ahead)
        else:
            sends[0][:, lanes(c)] = ahead[:k]
            sends[2][:, lanes(c)] = back


def form_kernel(
    y_ref,
    z_ref,
    dinv_ref,
    blocks_ref,
    partner_ref,
    landing_ref,
    pay_inner_ref,
    pay_outer_ref,
    col_ref,
    tgt_ref,
    count_ref,
    right_ref,
    sums_ref,
    parts_ref,
    acc,
):
    rb = z_ref.shape[0]
    k, nodes = y_ref.shape
    acc[...] = jnp.zeros_like(acc)
    count = count_ref[0]
    rows, _, _ = payload_rows(k)
    for c in range(CROSS):
        weights = jnp.where(even_group(), pay_outer_ref[rows[c]], pay_inner_ref[rows[c]])
        right_ref[:, lanes(rb + c)] = split(fold(times(landing_ref[:, lanes(c)], weights), k))
    for c in range(CROSS, blocks_ref.shape[0]):
        forward = fold(times_t(z_ref[col_ref[c]], blocks_ref[c]), k)
        acc[jnp.where(c < count, tgt_ref[c], rb)] += forward
    mine = side_by_side(z_ref)
    for at in range(0, nodes, WIDE):
        ids = lax.broadcasted_iota(jnp.int32, (WIDE, nodes), 0) + at
        onehot = jnp.where(ids == partner_ref[...], 0.5, 0.0).astype(BF16)
        right_ref[:, at : at + WIDE] = times_t(mine, onehot).astype(BF16)
    for j in range(rb):
        parts_ref[:, lanes(j)] = split(y_ref[:, lanes(j)])
    near = [split(acc[j] * dinv_ref[:, lanes(j)]) for j in range(rb)]
    parts = parts_ref[...]
    left = jnp.concatenate([parts, jnp.concatenate(near, axis=1)], axis=0)
    both = halves_added(times_t(left, parts))
    sums_ref[:, :k] = both[:k]
    sums_ref[:, k:] = both[k:]


def halves_added(product):
    k = product.shape[1] // 2
    wide = product[:, :k] + product[:, k:]
    pairs = range(0, product.shape[0], 2 * k)
    return jnp.concatenate([wide[at : at + k] + wide[at + k : at + 2 * k] for at in pairs], axis=0)


def pair_kernel(right_ref, sums_ref, prev_ref, part_ref, out_ref):
    k = sums_ref.shape[0]
    theirs = jnp.concatenate([side_by_side(part_ref), prev_ref[...]], axis=1)
    product = times_t(theirs, right_ref[...])
    form = product[:, :k] + product[:, k:]
    both = sums_ref[...] + jnp.concatenate([jnp.zeros((k, k), F32), form], axis=1)
    rows = out_ref.shape[1]
    for g in range(out_ref.shape[0]):
        out_ref[g] = both[g * rows : (g + 1) * rows]


def inverse_factor(gram):
    k = gram.shape[0]
    row_ids = lax.broadcasted_iota(jnp.int32, (SUBLANES, 2 * k), 0)
    lane = lax.broadcasted_iota(jnp.int32, (SUBLANES, 2 * k), 1)
    padded = jnp.concatenate([gram, jnp.zeros((k, k), F32)], axis=1)
    tiles = []
    for t in range(k // SUBLANES):
        tile = padded[t * SUBLANES : (t + 1) * SUBLANES]
        tiles.append(jnp.where(lane == row_ids + (k + t * SUBLANES), 1.0, tile))
    for start in range(0, k, PANEL):
        top, offset = divmod(start, SUBLANES)
        below = range(top, len(tiles))
        columns, rows = [], []
        for j in range(PANEL):
            at = start + j
            columns.append(
                {t: jnp.broadcast_to(tiles[t][:, at : at + 1], (SUBLANES, 2 * k)) for t in below}
            )
            rows.append(tiles[top][offset + j : offset + j + 1])
        for j in range(PANEL):
            pivot = lax.rsqrt(columns[j][top][offset + j : offset + j + 1])
            rows[j] = rows[j] * pivot
            columns[j] = {t: c * pivot for t, c in columns[j].items()}
            for m in range(j + 1, PANEL):
                factor = columns[j][top][offset + m : offset + m + 1]
                rows[m] = rows[m] - rows[j] * factor
                columns[m] = {t: c - columns[j][t] * factor for t, c in columns[m].items()}
        for t in below:
            if t == top and offset + PANEL == SUBLANES:
                continue
            tile = tiles[t]
            for j in range(PANEL):
                tile = tile - columns[j][t] * rows[j]
            if t == top:
                tile = jnp.where(row_ids >= offset + PANEL, tile, tiles[t])
            tiles[t] = tile
        for j in range(PANEL):
            tiles[top] = jnp.where(row_ids == offset + j, rows[j], tiles[top])
    return jnp.concatenate([tile[:, k:] for tile in tiles], axis=0)


def solve_kernel(nodes, both_ref, parts_ref, sub_ref, ray_ref):
    k = sub_ref.shape[0]
    pieces, _, _ = both_ref.shape
    both = jnp.concatenate([both_ref[g] for g in range(pieces)], axis=0) * (1.0 / nodes)
    gram = both[:, :k]
    form = both[:, k:]
    projected = gram + form + form.T
    inverse = inverse_factor(gram)
    left = split(inverse)
    sub_ref[...] = fold(times(jnp.concatenate([left, left], axis=1), parts_ref[...]), k)
    half = fold(times(jnp.concatenate([left, left], axis=1), split(projected)), k)
    ray_ref[...] = halves_added(times_t(split(half), left))


def call(kernel, ins, outs, scratch, *args, out_specs=None, cost=None):
    return pl.pallas_call(
        kernel,
        out_shape=[jax.ShapeDtypeStruct(shape, dtype) for shape, dtype in outs],
        in_specs=ins,
        out_specs=[VMEM] * len(outs) if out_specs is None else out_specs,
        scratch_shapes=scratch,
        cost_estimate=cost,
        compiler_params=pltpu.CompilerParams(vmem_limit_bytes=24 * 1024 * 1024),
    )(*args)


def shards(start_block, blocks, block_column, block_target, block_count, partner, degree):
    k, nodes = start_block.shape
    rb = nodes // BLOCK
    blk, scale = lax.axis_size("blk"), lax.axis_size("scale")
    node_total = nodes * blk * scale
    degree = degree.reshape(1, nodes)
    partner = partner.reshape(1, nodes)

    def moved(array, target):
        return lax.ppermute(array, "blk", [(i, target(i) % blk) for i in range(blk)])

    def swapped(array):
        return lax.ppermute(array, "scale", [(i, i ^ 1) for i in range(scale)])

    def inner(i):
        return i + 1 - 2 * (i % 2)

    def outer(i):
        return i - 1 + 2 * (i % 2)

    dinv, scaled, to_inner, to_outer, column, target = call(
        first_kernel,
        [pl.BlockSpec(memory_space=pltpu.HBM)] * 5,
        [
            ((1, nodes), F32),
            ((rb, k, BLOCK), BF16),
            ((rb * k, BLOCK), BF16),
            ((rb * k, BLOCK), BF16),
            (block_column.shape, jnp.int32),
            (block_target.shape, jnp.int32),
        ],
        [
            pltpu.VMEM((k, nodes), F32),
            pltpu.VMEM((1, nodes), jnp.int32),
            pltpu.VMEM((rb * k, BLOCK), BF16),
            pltpu.SemaphoreType.DMA((6,)),
        ],
        *[
            pltpu.with_memory_space_constraint(array, pltpu.HBM)
            for array in (start_block, degree, blocks, block_column, block_target)
        ],
        out_specs=[VMEM] * 4 + [SMEM] * 2,
        cost=pl.CostEstimate(flops=0, transcendentals=0, bytes_accessed=1 << 26),
    )

    def near(z):
        return call(
            near_kernel,
            [VMEM, VMEM, SMEM, SMEM, SMEM],
            [((rb, k, BLOCK), F32)],
            [pltpu.VMEM((rb + 1, k, BLOCK), F32)],
            z,
            blocks,
            column,
            target,
            block_count,
        )[0]

    def finish(first, near_sum, v, from_inner, from_outer, part):
        outs = [((k, nodes), F32), ((rb, 2 * k, BLOCK), BF16)]
        if first:
            outs += [((2 * k, CROSS * BLOCK), BF16)] * 2
        else:
            outs += [((k, CROSS * BLOCK), BF16), ((rb, k, BLOCK), BF16)]
            outs += [((2 * k, CROSS * BLOCK), BF16)]
        return call(
            functools.partial(finish_kernel, first),
            [VMEM] * 10 + [SMEM, SMEM],
            outs,
            [pltpu.VMEM((rb, k, BLOCK), F32)],
            near_sum,
            v,
            dinv,
            from_inner,
            from_outer,
            pay_inner,
            pay_outer,
            part,
            partner,
            blocks,
            column,
            target,
        )

    pay_outer = moved(to_outer, outer)
    pay_inner = moved(to_inner, inner)
    part = swapped(scaled)
    first_image, z, to_inner, to_outer = finish(
        True, near(scaled), start_block, pay_inner, pay_outer, part
    )

    from_outer = moved(to_outer, outer)
    from_inner = moved(to_inner, inner)
    part = swapped(z)
    images, z, ahead, high, landing = finish(False, near(z), first_image, from_inner, from_outer, part)

    from_prev = moved(ahead, lambda i: i + 1)
    part = swapped(high)
    right, sums, parts = call(
        form_kernel,
        [VMEM] * 8 + [SMEM] * 3,
        [((2 * k, nodes + CROSS * BLOCK), BF16), ((k, 2 * k), F32), ((2 * k, nodes), BF16)],
        [pltpu.VMEM((rb + 1, k, BLOCK), F32)],
        images,
        z,
        dinv,
        blocks,
        partner,
        landing,
        pay_inner,
        pay_outer,
        column,
        target,
        block_count,
    )
    plane = ALONG_X * scale
    depth = blk // ALONG_X
    rows = k // plane
    (mine,) = call(
        pair_kernel,
        [VMEM] * 4,
        [((plane, rows, 2 * k), F32)],
        [],
        right,
        sums,
        from_prev,
        part,
    )

    planes = [[z_at * plane + i for i in range(plane)] for z_at in range(depth)]
    columns = [[z_at * ALONG_X + x_at for z_at in range(depth)] for x_at in range(ALONG_X)]
    piece = lax.all_to_all(mine, BOTH, 0, 0, axis_index_groups=planes).sum(0)
    piece = jnp.broadcast_to(piece[None], (depth, rows, 2 * k))
    piece = lax.all_to_all(piece, "blk", 0, 0, axis_index_groups=columns).sum(0)
    piece = jnp.broadcast_to(piece[None], (plane, rows, 2 * k))
    both = lax.all_to_all(piece, BOTH, 0, 0, axis_index_groups=planes)

    return call(
        functools.partial(solve_kernel, node_total),
        [VMEM, VMEM],
        [((k, nodes), F32), ((k, k), F32)],
        [],
        both,
        parts,
    )


def layered(*args):
    return tuple(shards(*args))


def solution(mesh):
    return jax.shard_map(
        layered,
        mesh=mesh,
        in_specs=(
            P(None, BOTH),
            P(BOTH, None, None),
            P(BOTH),
            P(BOTH),
            P(BOTH),
            P(BOTH),
            P(BOTH),
        ),
        out_specs=(P(None, BOTH), P()),
        check_vma=False,
    )
```

```python
import functools

import jax
import jax.numpy as jnp
from jax import lax
from jax.experimental import pallas as pl
from jax.experimental.pallas import tpu as pltpu
from jax.sharding import PartitionSpec as P


BLOCK = 128
CROSS = 2
ALONG_X = 4
SUBLANES = 8
TILE_ROWS = 16
WIDE = 256
PANEL = 8
BOTH = ("blk", "scale")
F32 = jnp.float32
BF16 = jnp.bfloat16

VMEM = pl.BlockSpec(memory_space=pltpu.VMEM)
SMEM = pl.BlockSpec(memory_space=pltpu.SMEM)


def lanes(j):
    return slice(j * BLOCK, (j + 1) * BLOCK)


def times(left, right):
    return jnp.dot(left, right, preferred_element_type=F32)


def times_t(left, right, precision=None):
    return lax.dot_general(
        left, right, (((1,), (1,)), ((), ())), precision=precision, preferred_element_type=F32
    )


def fold(product, k):
    return product if product.shape[0] == k else product[:k] + product[k:]


def split(value):
    high = value.astype(BF16)
    return jnp.concatenate([high, (value - high.astype(F32)).astype(BF16)], axis=0)


def even_group():
    return lax.rem(lax.axis_index("blk"), 2) == 0


def first_kernel(
    x_hbm,
    degree_hbm,
    blocks_hbm,
    col_hbm,
    tgt_hbm,
    dinv_ref,
    scaled_ref,
    inner_ref,
    outer_ref,
    col_ref,
    tgt_ref,
    x_ref,
    degree_ref,
    ahead_ref,
    sems,
):
    rb, k, _ = scaled_ref.shape
    rows, picks, places = payload_rows(k)
    moves = [
        (degree_hbm, degree_ref),
        (x_hbm, x_ref),
        (col_hbm, col_ref),
        (tgt_hbm, tgt_ref),
    ]
    moves += [(blocks_hbm.at[c], ahead_ref.at[rows[c]]) for c in range(CROSS)]
    copies = [pltpu.make_async_copy(src, dst, sems.at[i]) for i, (src, dst) in enumerate(moves)]
    for copy in copies:
        copy.start()
    for copy in copies[:2]:
        copy.wait()
    dinv = 1.0 / jnp.sqrt(degree_ref[...].astype(F32))
    dinv_ref[...] = dinv
    for j in range(rb):
        scaled_ref[j] = (x_ref[:, lanes(j)] * dinv[:, lanes(j)]).astype(BF16)
    tail = places[-1].stop
    ahead_ref[tail:] = jnp.zeros_like(ahead_ref[tail:])
    for copy in copies[2:]:
        copy.wait()
    for c in range(CROSS):
        ahead_ref[picks[c]] = scaled_ref[col_ref[c]]
        place = jnp.full((TILE_ROWS, BLOCK), tgt_ref[c] - rb, jnp.int32)
        ahead_ref[places[c]] = place.astype(F32).astype(BF16)
    even = even_group()
    ahead = ahead_ref[...]
    back = jnp.concatenate([scaled_ref[j] for j in range(rb)], axis=0)
    inner_ref[...] = jnp.where(even, ahead, back)
    outer_ref[...] = jnp.where(even, back, ahead)


def payload_rows(k):
    sizes = [BLOCK] * CROSS + [k] * CROSS + [TILE_ROWS] * CROSS
    starts = [sum(sizes[:i]) for i in range(len(sizes))]
    spans = [slice(at, at + size) for at, size in zip(starts, sizes)]
    return spans[:CROSS], spans[CROSS : 2 * CROSS], spans[2 * CROSS :]


def diagonal(z_ref, place_ref, slots):
    first, second = z_ref[place_ref[slots[0]]], z_ref[place_ref[slots[1]]]
    zero = jnp.zeros_like(first)
    return jnp.concatenate(
        [jnp.concatenate([first, zero], axis=1), jnp.concatenate([zero, second], axis=1)], axis=0
    )


def across(blocks_ref, slots):
    return jnp.concatenate([blocks_ref[c] for c in slots], axis=1)


def down(blocks_ref, slots):
    return jnp.concatenate([blocks_ref[c] for c in slots], axis=0)


def near_kernel(z_ref, blocks_ref, col_ref, tgt_ref, count_ref, out_ref, acc):
    rb, k, _ = out_ref.shape
    acc[...] = jnp.zeros_like(acc)
    count = count_ref[0]
    slots = range(CROSS, blocks_ref.shape[0])

    def add(c, forward, backward):
        live = c < count
        acc[jnp.where(live, tgt_ref[c], rb)] += forward
        acc[jnp.where(live, col_ref[c], rb)] += backward

    if z_ref.shape[1] == k:
        for c in slots[::2]:
            pair = (c, c + 1)
            forward = times_t(diagonal(z_ref, col_ref, pair), across(blocks_ref, pair))
            backward = times(diagonal(z_ref, tgt_ref, pair), down(blocks_ref, pair))
            add(c, forward[:k], backward[:k])
            add(c + 1, forward[k:], backward[k:])
    else:
        for c in slots:
            weights = blocks_ref[c]
            forward = fold(times_t(z_ref[col_ref[c]], weights), k)
            add(c, forward, fold(times(z_ref[tgt_ref[c]], weights), k))
    for j in range(rb):
        out_ref[j] = acc[j]


def side_by_side(ref):
    return jnp.concatenate([ref[j] for j in range(ref.shape[0])], axis=1)


def crossed_blocks(part_ref, partner_ref, at, k):
    nodes = partner_ref.shape[1]
    ids = lax.broadcasted_iota(jnp.int32, (nodes, WIDE), 0)
    onehot = jnp.where(ids == partner_ref[:, at : at + WIDE], 1.0, 0.0).astype(BF16)
    return fold(times(side_by_side(part_ref), onehot), k)


def cross_kernel(near_ref, part_ref, partner_ref, out_ref):
    rb, k, _ = near_ref.shape
    for at in range(0, rb * BLOCK, WIDE):
        crossed = crossed_blocks(part_ref, partner_ref, at, k)
        for i in range(WIDE // BLOCK):
            j = at // BLOCK + i
            out_ref[j] = near_ref[j] + crossed[:, lanes(i)]


def finish_kernel(
    first,
    near_ref,
    v_ref,
    dinv_ref,
    inner_ref,
    outer_ref,
    pay_inner_ref,
    pay_outer_ref,
    blocks_ref,
    col_ref,
    tgt_ref,
    y_ref,
    z_ref,
    *rest,
):
    *sends, tot = rest
    k = v_ref.shape[0]
    rb = v_ref.shape[1] // BLOCK
    even = even_group()
    for j in range(rb):
        tot[j] = near_ref[j]
    rows, picks, spots = payload_rows(k)
    places = []
    for c in range(CROSS):
        sent = jnp.where(even, pay_outer_ref[spots[c]], pay_inner_ref[spots[c]])
        places.append(jnp.max(sent.astype(F32)).astype(jnp.int32))
        if first:
            at = pl.ds(pl.multiple_of((tgt_ref[c] - rb) * k, k), k)
            theirs = jnp.where(even, inner_ref[at], outer_ref[at])
            behind = jnp.where(even, pay_outer_ref[picks[c]], pay_inner_ref[picks[c]])
        else:
            theirs = jnp.where(even, inner_ref[:, lanes(c)], outer_ref[:, lanes(c)])
            behind = jnp.where(even, outer_ref[:, lanes(c)], inner_ref[:, lanes(c)])
        weights = jnp.where(even, pay_outer_ref[rows[c]], pay_inner_ref[rows[c]])
        tot[col_ref[c]] += fold(times(theirs, blocks_ref[c]), k)
        landed = fold(times_t(behind, weights), k)
        tot[places[c]] += landed
    for j in range(rb):
        dinv = dinv_ref[:, lanes(j)]
        y = v_ref[:, lanes(j)] + dinv * tot[j]
        y_ref[:, lanes(j)] = y
        z_ref[j] = split(y * dinv)
        if not first:
            sends[1][j] = z_ref[j, :k]
    for c in range(CROSS):
        back = z_ref[places[c]]
        ahead = z_ref[col_ref[c]]
        if first:
            sends[0][:, lanes(c)] = jnp.where(even, ahead[:k], back[:k])
            sends[1][:, lanes(c)] = jnp.where(even, back[:k], ahead[:k])
        else:
            sends[0][:, lanes(c)] = ahead[:k]
            sends[2][:, lanes(c)] = back


def form_kernel(
    y_ref,
    z_ref,
    dinv_ref,
    blocks_ref,
    partner_ref,
    landing_ref,
    pay_inner_ref,
    pay_outer_ref,
    col_ref,
    tgt_ref,
    count_ref,
    right_ref,
    sums_ref,
    parts_ref,
    acc,
):
    rb = z_ref.shape[0]
    k, nodes = y_ref.shape
    acc[...] = jnp.zeros_like(acc)
    count = count_ref[0]
    rows, _, _ = payload_rows(k)
    for c in range(CROSS):
        weights = jnp.where(even_group(), pay_outer_ref[rows[c]], pay_inner_ref[rows[c]])
        right_ref[:, lanes(rb + c)] = split(fold(times(landing_ref[:, lanes(c)], weights), k))
    for c in range(CROSS, blocks_ref.shape[0]):
        forward = fold(times_t(z_ref[col_ref[c]], blocks_ref[c]), k)
        acc[jnp.where(c < count, tgt_ref[c], rb)] += forward
    mine = side_by_side(z_ref)
    for at in range(0, nodes, WIDE):
        ids = lax.broadcasted_iota(jnp.int32, (WIDE, nodes), 0) + at
        onehot = jnp.where(ids == partner_ref[...], 0.5, 0.0).astype(BF16)
        right_ref[:, at : at + WIDE] = times_t(mine, onehot).astype(BF16)
    for j in range(rb):
        parts_ref[:, lanes(j)] = split(y_ref[:, lanes(j)])
    near = [split(acc[j] * dinv_ref[:, lanes(j)]) for j in range(rb)]
    parts = parts_ref[...]
    left = jnp.concatenate([parts, jnp.concatenate(near, axis=1)], axis=0)
    both = halves_added(times_t(left, parts))
    sums_ref[:, :k] = both[:k]
    sums_ref[:, k:] = both[k:]


def halves_added(product):
    k = product.shape[1] // 2
    wide = product[:, :k] + product[:, k:]
    pairs = range(0, product.shape[0], 2 * k)
    return jnp.concatenate([wide[at : at + k] + wide[at + k : at + 2 * k] for at in pairs], axis=0)


def pair_kernel(right_ref, sums_ref, prev_ref, part_ref, out_ref):
    k = sums_ref.shape[0]
    theirs = jnp.concatenate([side_by_side(part_ref), prev_ref[...]], axis=1)
    product = times_t(theirs, right_ref[...])
    form = product[:, :k] + product[:, k:]
    both = sums_ref[...] + jnp.concatenate([jnp.zeros((k, k), F32), form], axis=1)
    rows = out_ref.shape[1]
    for g in range(out_ref.shape[0]):
        out_ref[g] = both[g * rows : (g + 1) * rows]


def inverse_factor(gram):
    k = gram.shape[0]
    row_ids = lax.broadcasted_iota(jnp.int32, (SUBLANES, 2 * k), 0)
    lane = lax.broadcasted_iota(jnp.int32, (SUBLANES, 2 * k), 1)
    padded = jnp.concatenate([gram, jnp.zeros((k, k), F32)], axis=1)
    tiles = []
    for t in range(k // SUBLANES):
        tile = padded[t * SUBLANES : (t + 1) * SUBLANES]
        tiles.append(jnp.where(lane == row_ids + (k + t * SUBLANES), 1.0, tile))
    for start in range(0, k, PANEL):
        top, offset = divmod(start, SUBLANES)
        below = range(top, len(tiles))
        columns, rows = [], []
        for j in range(PANEL):
            at = start + j
            columns.append(
                {t: jnp.broadcast_to(tiles[t][:, at : at + 1], (SUBLANES, 2 * k)) for t in below}
            )
            rows.append(tiles[top][offset + j : offset + j + 1])
        for j in range(PANEL):
            pivot = lax.rsqrt(columns[j][top][offset + j : offset + j + 1])
            rows[j] = rows[j] * pivot
            columns[j] = {t: c * pivot for t, c in columns[j].items()}
            for m in range(j + 1, PANEL):
                factor = columns[j][top][offset + m : offset + m + 1]
                rows[m] = rows[m] - rows[j] * factor
                columns[m] = {t: c - columns[j][t] * factor for t, c in columns[m].items()}
        for t in below:
            if t == top and offset + PANEL == SUBLANES:
                continue
            tile = tiles[t]
            for j in range(PANEL):
                tile = tile - columns[j][t] * rows[j]
            if t == top:
                tile = jnp.where(row_ids >= offset + PANEL, tile, tiles[t])
            tiles[t] = tile
        for j in range(PANEL):
            tiles[top] = jnp.where(row_ids == offset + j, rows[j], tiles[top])
    return jnp.concatenate([tile[:, k:] for tile in tiles], axis=0)


def solve_kernel(nodes, both_ref, parts_ref, sub_ref, ray_ref):
    k = sub_ref.shape[0]
    pieces, _, _ = both_ref.shape
    both = jnp.concatenate([both_ref[g] for g in range(pieces)], axis=0) * (1.0 / nodes)
    gram = both[:, :k]
    form = both[:, k:]
    projected = gram + form + form.T
    inverse = inverse_factor(gram)
    left = split(inverse)
    sub_ref[...] = fold(times(jnp.concatenate([left, left], axis=1), parts_ref[...]), k)
    half = fold(times(jnp.concatenate([left, left], axis=1), split(projected)), k)
    ray_ref[...] = halves_added(times_t(split(half), left))


def call(kernel, ins, outs, scratch, *args, out_specs=None, cost=None):
    return pl.pallas_call(
        kernel,
        out_shape=[jax.ShapeDtypeStruct(shape, dtype) for shape, dtype in outs],
        in_specs=ins,
        out_specs=[VMEM] * len(outs) if out_specs is None else out_specs,
        scratch_shapes=scratch,
        cost_estimate=cost,
        compiler_params=pltpu.CompilerParams(vmem_limit_bytes=24 * 1024 * 1024),
    )(*args)


def shards(start_block, blocks, block_column, block_target, block_count, partner, degree):
    k, nodes = start_block.shape
    rb = nodes // BLOCK
    blk, scale = lax.axis_size("blk"), lax.axis_size("scale")
    node_total = nodes * blk * scale
    degree = degree.reshape(1, nodes)
    partner = partner.reshape(1, nodes)

    def moved(array, target):
        return lax.ppermute(array, "blk", [(i, target(i) % blk) for i in range(blk)])

    def swapped(array):
        return lax.ppermute(array, "scale", [(i, i ^ 1) for i in range(scale)])

    def inner(i):
        return i + 1 - 2 * (i % 2)

    def outer(i):
        return i - 1 + 2 * (i % 2)

    dinv, scaled, to_inner, to_outer, column, target = call(
        first_kernel,
        [pl.BlockSpec(memory_space=pltpu.HBM)] * 5,
        [
            ((1, nodes), F32),
            ((rb, k, BLOCK), BF16),
            ((rb * k, BLOCK), BF16),
            ((rb * k, BLOCK), BF16),
            (block_column.shape, jnp.int32),
            (block_target.shape, jnp.int32),
        ],
        [
            pltpu.VMEM((k, nodes), F32),
            pltpu.VMEM((1, nodes), jnp.int32),
            pltpu.VMEM((rb * k, BLOCK), BF16),
            pltpu.SemaphoreType.DMA((6,)),
        ],
        *[
            pltpu.with_memory_space_constraint(array, pltpu.HBM)
            for array in (start_block, degree, blocks, block_column, block_target)
        ],
        out_specs=[VMEM] * 4 + [SMEM] * 2,
        cost=pl.CostEstimate(flops=0, transcendentals=0, bytes_accessed=1 << 26),
    )

    def near(z):
        return call(
            near_kernel,
            [VMEM, VMEM, SMEM, SMEM, SMEM],
            [((rb, k, BLOCK), F32)],
            [pltpu.VMEM((rb + 1, k, BLOCK), F32)],
            z,
            blocks,
            column,
            target,
            block_count,
        )[0]

    def finish(first, near_sum, v, from_inner, from_outer, part):
        (near_sum,) = call(
            cross_kernel,
            [VMEM] * 3,
            [((rb, k, BLOCK), F32)],
            [],
            near_sum,
            part,
            partner,
        )
        outs = [((k, nodes), F32), ((rb, 2 * k, BLOCK), BF16)]
        if first:
            outs += [((k, CROSS * BLOCK), BF16)] * 2
        else:
            outs += [((k, CROSS * BLOCK), BF16), ((rb, k, BLOCK), BF16)]
            outs += [((2 * k, CROSS * BLOCK), BF16)]
        return call(
            functools.partial(finish_kernel, first),
            [VMEM] * 8 + [SMEM, SMEM],
            outs,
            [pltpu.VMEM((rb, k, BLOCK), F32)],
            near_sum,
            v,
            dinv,
            from_inner,
            from_outer,
            pay_inner,
            pay_outer,
            blocks,
            column,
            target,
        )

    pay_outer = moved(to_outer, outer)
    pay_inner = moved(to_inner, inner)
    part = swapped(scaled)
    first_image, z, to_inner, to_outer = finish(
        True, near(scaled), start_block, pay_inner, pay_outer, part
    )

    from_outer = moved(to_outer, outer)
    from_inner = moved(to_inner, inner)
    part = swapped(z)
    images, z, ahead, high, landing = finish(False, near(z), first_image, from_inner, from_outer, part)

    from_prev = moved(ahead, lambda i: i + 1)
    part = swapped(high)
    right, sums, parts = call(
        form_kernel,
        [VMEM] * 8 + [SMEM] * 3,
        [((2 * k, nodes + CROSS * BLOCK), BF16), ((k, 2 * k), F32), ((2 * k, nodes), BF16)],
        [pltpu.VMEM((rb + 1, k, BLOCK), F32)],
        images,
        z,
        dinv,
        blocks,
        partner,
        landing,
        pay_inner,
        pay_outer,
        column,
        target,
        block_count,
    )
    plane = ALONG_X * scale
    depth = blk // ALONG_X
    rows = k // plane
    (mine,) = call(
        pair_kernel,
        [VMEM] * 4,
        [((plane, rows, 2 * k), F32)],
        [],
        right,
        sums,
        from_prev,
        part,
    )

    planes = [[z_at * plane + i for i in range(plane)] for z_at in range(depth)]
    columns = [[z_at * ALONG_X + x_at for z_at in range(depth)] for x_at in range(ALONG_X)]
    piece = lax.all_to_all(mine, BOTH, 0, 0, axis_index_groups=planes).sum(0)
    piece = jnp.broadcast_to(piece[None], (depth, rows, 2 * k))
    piece = lax.all_to_all(piece, "blk", 0, 0, axis_index_groups=columns).sum(0)
    piece = jnp.broadcast_to(piece[None], (plane, rows, 2 * k))
    both = lax.all_to_all(piece, BOTH, 0, 0, axis_index_groups=planes)

    return call(
        functools.partial(solve_kernel, node_total),
        [VMEM, VMEM],
        [((k, nodes), F32), ((k, k), F32)],
        [],
        both,
        parts,
    )


def layered(*args):
    return tuple(shards(*args))


def solution(mesh):
    return jax.shard_map(
        layered,
        mesh=mesh,
        in_specs=(
            P(None, BOTH),
            P(BOTH, None, None),
            P(BOTH),
            P(BOTH),
            P(BOTH),
            P(BOTH),
            P(BOTH),
        ),
        out_specs=(P(None, BOTH), P()),
        check_vma=False,
    )
```

```python
import functools

import jax
import jax.numpy as jnp
from jax import lax
from jax.experimental import pallas as pl
from jax.experimental.pallas import tpu as pltpu
from jax.sharding import PartitionSpec as P


BLOCK = 128
CROSS = 2
ALONG_X = 4
SUBLANES = 8
TILE_ROWS = 16
WIDE = 256
PANEL = 8
BOTH = ("blk", "scale")
F32 = jnp.float32
BF16 = jnp.bfloat16

VMEM = pl.BlockSpec(memory_space=pltpu.VMEM)
SMEM = pl.BlockSpec(memory_space=pltpu.SMEM)


def lanes(j):
    return slice(j * BLOCK, (j + 1) * BLOCK)


def times(left, right):
    return jnp.dot(left, right, preferred_element_type=F32)


def times_t(left, right, precision=None):
    return lax.dot_general(
        left, right, (((1,), (1,)), ((), ())), precision=precision, preferred_element_type=F32
    )


def fold(product, k):
    return product if product.shape[0] == k else product[:k] + product[k:]


def split(value):
    high = value.astype(BF16)
    return jnp.concatenate([high, (value - high.astype(F32)).astype(BF16)], axis=0)


def even_group():
    return lax.rem(lax.axis_index("blk"), 2) == 0


def first_kernel(
    x_hbm,
    degree_hbm,
    blocks_hbm,
    col_hbm,
    tgt_hbm,
    dinv_ref,
    scaled_ref,
    inner_ref,
    outer_ref,
    col_ref,
    tgt_ref,
    x_ref,
    degree_ref,
    ahead_ref,
    sems,
):
    rb, k, _ = scaled_ref.shape
    rows, picks, places = payload_rows(k)
    moves = [
        (degree_hbm, degree_ref),
        (x_hbm, x_ref),
        (col_hbm, col_ref),
        (tgt_hbm, tgt_ref),
    ]
    moves += [(blocks_hbm.at[c], ahead_ref.at[rows[c]]) for c in range(CROSS)]
    copies = [pltpu.make_async_copy(src, dst, sems.at[i]) for i, (src, dst) in enumerate(moves)]
    for copy in copies:
        copy.start()
    for copy in copies[:2]:
        copy.wait()
    dinv = 1.0 / jnp.sqrt(degree_ref[...].astype(F32))
    dinv_ref[...] = dinv
    for j in range(rb):
        scaled_ref[j] = (x_ref[:, lanes(j)] * dinv[:, lanes(j)]).astype(BF16)
    tail = places[-1].stop
    ahead_ref[tail:] = jnp.zeros_like(ahead_ref[tail:])
    for copy in copies[2:]:
        copy.wait()
    for c in range(CROSS):
        ahead_ref[picks[c]] = scaled_ref[col_ref[c]]
        place = jnp.full((TILE_ROWS, BLOCK), tgt_ref[c] - rb, jnp.int32)
        ahead_ref[places[c]] = place.astype(F32).astype(BF16)
    even = even_group()
    ahead = ahead_ref[...]
    back = jnp.concatenate([scaled_ref[j] for j in range(rb)], axis=0)
    inner_ref[...] = jnp.where(even, ahead, back)
    outer_ref[...] = jnp.where(even, back, ahead)


def payload_rows(k):
    sizes = [BLOCK] * CROSS + [k] * CROSS + [TILE_ROWS] * CROSS
    starts = [sum(sizes[:i]) for i in range(len(sizes))]
    spans = [slice(at, at + size) for at, size in zip(starts, sizes)]
    return spans[:CROSS], spans[CROSS : 2 * CROSS], spans[2 * CROSS :]


def diagonal(z_ref, place_ref, slots):
    first, second = z_ref[place_ref[slots[0]]], z_ref[place_ref[slots[1]]]
    zero = jnp.zeros_like(first)
    return jnp.concatenate(
        [jnp.concatenate([first, zero], axis=1), jnp.concatenate([zero, second], axis=1)], axis=0
    )


def across(blocks_ref, slots):
    return jnp.concatenate([blocks_ref[c] for c in slots], axis=1)


def down(blocks_ref, slots):
    return jnp.concatenate([blocks_ref[c] for c in slots], axis=0)


def near_kernel(z_ref, blocks_ref, col_ref, tgt_ref, count_ref, out_ref, acc):
    rb, k, _ = out_ref.shape
    acc[...] = jnp.zeros_like(acc)
    count = count_ref[0]
    slots = range(CROSS, blocks_ref.shape[0])

    def add(c, forward, backward):
        live = c < count
        acc[jnp.where(live, tgt_ref[c], rb)] += forward
        acc[jnp.where(live, col_ref[c], rb)] += backward

    if z_ref.shape[1] == k:
        for c in slots[::2]:
            pair = (c, c + 1)
            forward = times_t(diagonal(z_ref, col_ref, pair), across(blocks_ref, pair))
            backward = times(diagonal(z_ref, tgt_ref, pair), down(blocks_ref, pair))
            add(c, forward[:k], backward[:k])
            add(c + 1, forward[k:], backward[k:])
    else:
        for c in slots:
            weights = blocks_ref[c]
            forward = fold(times_t(z_ref[col_ref[c]], weights), k)
            add(c, forward, fold(times(z_ref[tgt_ref[c]], weights), k))
    for j in range(rb):
        out_ref[j] = acc[j]


def side_by_side(ref):
    return jnp.concatenate([ref[j] for j in range(ref.shape[0])], axis=1)


def crossed_blocks(part_ref, partner_ref, at, k):
    nodes = partner_ref.shape[1]
    ids = lax.broadcasted_iota(jnp.int32, (nodes, WIDE), 0)
    onehot = jnp.where(ids == partner_ref[:, at : at + WIDE], 1.0, 0.0).astype(BF16)
    return fold(times(side_by_side(part_ref), onehot), k)


def cross_kernel(near_ref, part_ref, partner_ref, out_ref):
    rb, k, _ = near_ref.shape
    for at in range(0, rb * BLOCK, WIDE):
        crossed = crossed_blocks(part_ref, partner_ref, at, k)
        for i in range(WIDE // BLOCK):
            j = at // BLOCK + i
            out_ref[j] = near_ref[j] + crossed[:, lanes(i)]


def finish_kernel(
    first,
    near_ref,
    v_ref,
    dinv_ref,
    inner_ref,
    outer_ref,
    pay_inner_ref,
    pay_outer_ref,
    blocks_ref,
    col_ref,
    tgt_ref,
    y_ref,
    z_ref,
    *rest,
):
    *sends, tot = rest
    k = v_ref.shape[0]
    rb = v_ref.shape[1] // BLOCK
    even = even_group()
    for j in range(rb):
        tot[j] = near_ref[j]
    rows, picks, spots = payload_rows(k)
    places = []
    for c in range(CROSS):
        sent = jnp.where(even, pay_outer_ref[spots[c]], pay_inner_ref[spots[c]])
        places.append(jnp.max(sent.astype(F32)).astype(jnp.int32))
        if first:
            at = pl.ds(pl.multiple_of((tgt_ref[c] - rb) * k, k), k)
            theirs = jnp.where(even, inner_ref[at], outer_ref[at])
            behind = jnp.where(even, pay_outer_ref[picks[c]], pay_inner_ref[picks[c]])
        else:
            theirs = jnp.where(even, inner_ref[:, lanes(c)], outer_ref[:, lanes(c)])
            behind = jnp.where(even, outer_ref[:, lanes(c)], inner_ref[:, lanes(c)])
        weights = jnp.where(even, pay_outer_ref[rows[c]], pay_inner_ref[rows[c]])
        tot[col_ref[c]] += fold(times(theirs, blocks_ref[c]), k)
        landed = fold(times_t(behind, weights), k)
        tot[places[c]] += landed
    for j in range(rb):
        dinv = dinv_ref[:, lanes(j)]
        y = v_ref[:, lanes(j)] + dinv * tot[j]
        y_ref[:, lanes(j)] = y
        z_ref[j] = split(y * dinv)
        if not first:
            sends[1][j] = z_ref[j, :k]
    for c in range(CROSS):
        back = z_ref[places[c]]
        ahead = z_ref[col_ref[c]]
        if first:
            sends[0][:, lanes(c)] = jnp.where(even, ahead[:k], back[:k])
            sends[1][:, lanes(c)] = jnp.where(even, back[:k], ahead[:k])
        else:
            sends[0][:, lanes(c)] = ahead[:k]
            sends[2][:, lanes(c)] = back


def form_kernel(
    y_ref,
    z_ref,
    dinv_ref,
    blocks_ref,
    landing_ref,
    pay_inner_ref,
    pay_outer_ref,
    col_ref,
    tgt_ref,
    count_ref,
    right_ref,
    sums_ref,
    parts_ref,
    acc,
):
    rb = z_ref.shape[0]
    k = y_ref.shape[0]
    acc[...] = jnp.zeros_like(acc)
    count = count_ref[0]
    rows, _, _ = payload_rows(k)
    for c in range(CROSS):
        weights = jnp.where(even_group(), pay_outer_ref[rows[c]], pay_inner_ref[rows[c]])
        right_ref[:, lanes(c)] = split(fold(times(landing_ref[:, lanes(c)], weights), k))
    for c in range(CROSS, blocks_ref.shape[0]):
        forward = fold(times_t(z_ref[col_ref[c]], blocks_ref[c]), k)
        acc[jnp.where(c < count, tgt_ref[c], rb)] += forward
    for j in range(rb):
        parts_ref[:, lanes(j)] = split(y_ref[:, lanes(j)])
    near = [split(acc[j] * dinv_ref[:, lanes(j)]) for j in range(rb)]
    parts = parts_ref[...]
    left = jnp.concatenate([parts, jnp.concatenate(near, axis=1)], axis=0)
    both = halves_added(times_t(left, parts))
    sums_ref[:, :k] = both[:k]
    sums_ref[:, k:] = both[k:]


def halves_added(product):
    k = product.shape[1] // 2
    wide = product[:, :k] + product[:, k:]
    pairs = range(0, product.shape[0], 2 * k)
    return jnp.concatenate([wide[at : at + k] + wide[at + k : at + 2 * k] for at in pairs], axis=0)


def pairs_kernel(sums_ref, z_ref, part_ref, partner_ref, out_ref):
    k = sums_ref.shape[0]
    ats = range(0, partner_ref.shape[1], WIDE)
    crossed = [crossed_blocks(part_ref, partner_ref, at, k).astype(BF16) for at in ats]
    product = times_t(jnp.concatenate(crossed, axis=1), side_by_side(z_ref))
    out_ref[:, :k] = sums_ref[:, :k]
    out_ref[:, k:] = sums_ref[:, k:] + 0.5 * (product[:, :k] + product[:, k:])


def pair_kernel(right_ref, sums_ref, prev_ref, out_ref):
    k = sums_ref.shape[0]
    product = times_t(prev_ref[...], right_ref[...])
    form = product[:, :k] + product[:, k:]
    both = sums_ref[...] + jnp.concatenate([jnp.zeros((k, k), F32), form], axis=1)
    rows = out_ref.shape[1]
    for g in range(out_ref.shape[0]):
        out_ref[g] = both[g * rows : (g + 1) * rows]


def inverse_factor(gram):
    k = gram.shape[0]
    row_ids = lax.broadcasted_iota(jnp.int32, (SUBLANES, 2 * k), 0)
    lane = lax.broadcasted_iota(jnp.int32, (SUBLANES, 2 * k), 1)
    padded = jnp.concatenate([gram, jnp.zeros((k, k), F32)], axis=1)
    tiles = []
    for t in range(k // SUBLANES):
        tile = padded[t * SUBLANES : (t + 1) * SUBLANES]
        tiles.append(jnp.where(lane == row_ids + (k + t * SUBLANES), 1.0, tile))
    for start in range(0, k, PANEL):
        top, offset = divmod(start, SUBLANES)
        below = range(top, len(tiles))
        columns, rows = [], []
        for j in range(PANEL):
            at = start + j
            columns.append(
                {t: jnp.broadcast_to(tiles[t][:, at : at + 1], (SUBLANES, 2 * k)) for t in below}
            )
            rows.append(tiles[top][offset + j : offset + j + 1])
        for j in range(PANEL):
            pivot = lax.rsqrt(columns[j][top][offset + j : offset + j + 1])
            rows[j] = rows[j] * pivot
            columns[j] = {t: c * pivot for t, c in columns[j].items()}
            for m in range(j + 1, PANEL):
                factor = columns[j][top][offset + m : offset + m + 1]
                rows[m] = rows[m] - rows[j] * factor
                columns[m] = {t: c - columns[j][t] * factor for t, c in columns[m].items()}
        for t in below:
            if t == top and offset + PANEL == SUBLANES:
                continue
            tile = tiles[t]
            for j in range(PANEL):
                tile = tile - columns[j][t] * rows[j]
            if t == top:
                tile = jnp.where(row_ids >= offset + PANEL, tile, tiles[t])
            tiles[t] = tile
        for j in range(PANEL):
            tiles[top] = jnp.where(row_ids == offset + j, rows[j], tiles[top])
    return jnp.concatenate([tile[:, k:] for tile in tiles], axis=0)


def solve_kernel(nodes, both_ref, parts_ref, sub_ref, ray_ref):
    k = sub_ref.shape[0]
    pieces, _, _ = both_ref.shape
    both = jnp.concatenate([both_ref[g] for g in range(pieces)], axis=0) * (1.0 / nodes)
    gram = both[:, :k]
    form = both[:, k:]
    projected = gram + form + form.T
    inverse = inverse_factor(gram)
    left = split(inverse)
    sub_ref[...] = fold(times(jnp.concatenate([left, left], axis=1), parts_ref[...]), k)
    half = fold(times(jnp.concatenate([left, left], axis=1), split(projected)), k)
    ray_ref[...] = halves_added(times_t(split(half), left))


def call(kernel, ins, outs, scratch, *args, out_specs=None, cost=None):
    return pl.pallas_call(
        kernel,
        out_shape=[jax.ShapeDtypeStruct(shape, dtype) for shape, dtype in outs],
        in_specs=ins,
        out_specs=[VMEM] * len(outs) if out_specs is None else out_specs,
        scratch_shapes=scratch,
        cost_estimate=cost,
        compiler_params=pltpu.CompilerParams(vmem_limit_bytes=24 * 1024 * 1024),
    )(*args)


def shards(start_block, blocks, block_column, block_target, block_count, partner, degree):
    k, nodes = start_block.shape
    rb = nodes // BLOCK
    blk, scale = lax.axis_size("blk"), lax.axis_size("scale")
    node_total = nodes * blk * scale
    degree = degree.reshape(1, nodes)
    partner = partner.reshape(1, nodes)

    def moved(array, target):
        return lax.ppermute(array, "blk", [(i, target(i) % blk) for i in range(blk)])

    def swapped(array):
        return lax.ppermute(array, "scale", [(i, i ^ 1) for i in range(scale)])

    def inner(i):
        return i + 1 - 2 * (i % 2)

    def outer(i):
        return i - 1 + 2 * (i % 2)

    dinv, scaled, to_inner, to_outer, column, target = call(
        first_kernel,
        [pl.BlockSpec(memory_space=pltpu.HBM)] * 5,
        [
            ((1, nodes), F32),
            ((rb, k, BLOCK), BF16),
            ((rb * k, BLOCK), BF16),
            ((rb * k, BLOCK), BF16),
            (block_column.shape, jnp.int32),
            (block_target.shape, jnp.int32),
        ],
        [
            pltpu.VMEM((k, nodes), F32),
            pltpu.VMEM((1, nodes), jnp.int32),
            pltpu.VMEM((rb * k, BLOCK), BF16),
            pltpu.SemaphoreType.DMA((6,)),
        ],
        *[
            pltpu.with_memory_space_constraint(array, pltpu.HBM)
            for array in (start_block, degree, blocks, block_column, block_target)
        ],
        out_specs=[VMEM] * 4 + [SMEM] * 2,
        cost=pl.CostEstimate(flops=0, transcendentals=0, bytes_accessed=1 << 26),
    )

    def near(z):
        return call(
            near_kernel,
            [VMEM, VMEM, SMEM, SMEM, SMEM],
            [((rb, k, BLOCK), F32)],
            [pltpu.VMEM((rb + 1, k, BLOCK), F32)],
            z,
            blocks,
            column,
            target,
            block_count,
        )[0]

    def finish(first, near_sum, v, from_inner, from_outer, part):
        (near_sum,) = call(
            cross_kernel,
            [VMEM] * 3,
            [((rb, k, BLOCK), F32)],
            [],
            near_sum,
            part,
            partner,
        )
        outs = [((k, nodes), F32), ((rb, 2 * k, BLOCK), BF16)]
        if first:
            outs += [((k, CROSS * BLOCK), BF16)] * 2
        else:
            outs += [((k, CROSS * BLOCK), BF16), ((rb, k, BLOCK), BF16)]
            outs += [((2 * k, CROSS * BLOCK), BF16)]
        return call(
            functools.partial(finish_kernel, first),
            [VMEM] * 8 + [SMEM, SMEM],
            outs,
            [pltpu.VMEM((rb, k, BLOCK), F32)],
            near_sum,
            v,
            dinv,
            from_inner,
            from_outer,
            pay_inner,
            pay_outer,
            blocks,
            column,
            target,
        )

    pay_outer = moved(to_outer, outer)
    pay_inner = moved(to_inner, inner)
    part = swapped(scaled)
    first_image, z, to_inner, to_outer = finish(
        True, near(scaled), start_block, pay_inner, pay_outer, part
    )

    from_outer = moved(to_outer, outer)
    from_inner = moved(to_inner, inner)
    part = swapped(z)
    images, z, ahead, high, landing = finish(False, near(z), first_image, from_inner, from_outer, part)

    from_prev = moved(ahead, lambda i: i + 1)
    part = swapped(high)
    right, sums, parts = call(
        form_kernel,
        [VMEM] * 7 + [SMEM] * 3,
        [((2 * k, CROSS * BLOCK), BF16), ((k, 2 * k), F32), ((2 * k, nodes), BF16)],
        [pltpu.VMEM((rb + 1, k, BLOCK), F32)],
        images,
        z,
        dinv,
        blocks,
        landing,
        pay_inner,
        pay_outer,
        column,
        target,
        block_count,
    )
    plane = ALONG_X * scale
    depth = blk // ALONG_X
    rows = k // plane
    (sums,) = call(pairs_kernel, [VMEM] * 4, [((k, 2 * k), F32)], [], sums, z, part, partner)
    (mine,) = call(
        pair_kernel,
        [VMEM] * 3,
        [((plane, rows, 2 * k), F32)],
        [],
        right,
        sums,
        from_prev,
    )

    planes = [[z_at * plane + i for i in range(plane)] for z_at in range(depth)]
    columns = [[z_at * ALONG_X + x_at for z_at in range(depth)] for x_at in range(ALONG_X)]
    piece = lax.all_to_all(mine, BOTH, 0, 0, axis_index_groups=planes).sum(0)
    piece = jnp.broadcast_to(piece[None], (depth, rows, 2 * k))
    piece = lax.all_to_all(piece, "blk", 0, 0, axis_index_groups=columns).sum(0)
    piece = jnp.broadcast_to(piece[None], (plane, rows, 2 * k))
    both = lax.all_to_all(piece, BOTH, 0, 0, axis_index_groups=planes)

    return call(
        functools.partial(solve_kernel, node_total),
        [VMEM, VMEM],
        [((k, nodes), F32), ((k, k), F32)],
        [],
        both,
        parts,
    )


def layered(*args):
    return tuple(shards(*args))


def solution(mesh):
    return jax.shard_map(
        layered,
        mesh=mesh,
        in_specs=(
            P(None, BOTH),
            P(BOTH, None, None),
            P(BOTH),
            P(BOTH),
            P(BOTH),
            P(BOTH),
            P(BOTH),
        ),
        out_specs=(P(None, BOTH), P()),
        check_vma=False,
    )
```
